256 devices in a mesh: seq: 64 (over x_hi, z, y), head: 4 (over x_lo, core).
Axes of the slice: x: 4 (x_hi: 2, x_lo: 2; x = x_hi * 2 + x_lo), y: 4, z: 8, core: 2. Of those that a mesh axis runs over, the one named last changes fastest.
Arguments:
- queries: bfloat16 [8192, 3584], P('seq', 'head'), may hold values from -256 to 256
- key_codes: bfloat16 [8192, 512], P('seq', 'head'), may hold values from -4 to 4
- value_codes: bfloat16 [8192, 512], P('seq', 'head'), may hold values from -4 to 4
- kv_scales: float32 [2, 64, 4], P(None, 'seq', 'head'), may hold values from 0.5 to 2
- out_weight: bfloat16 [3584, 3584], P('head'), may hold values from -0.09375 to 0.09375
- turn_ids: int32 [8192], replicated, may hold values from 0 to 63, never falling along the last dimension, each value on 1 to 256 neighbouring positions
- block_mask: int32 [64, 64], P('seq'), may hold values 0 or 1
- doc_lengths: int32 [4], replicated, may hold values from 1 to 4096, 8192 in all
Outputs:
- projected: bfloat16 [8192, 3584], P('seq', 'head')
The draws below stay inside these ranges and needn't reach their ends.
All inputs are finite; a program needn't handle non-finite values. No bound on the sum of `block_mask` on one device may be relied on, other than what follows from the above.
Results may differ from the reference program's by a relative error of at most 0.012.
Values may be sent and summed in bfloat16 or wider, within the bound.
A program may use at most 128 MiB of HBM per device.

```python
import math
import jax
import jax.numpy as jnp
import numpy as np
from jax import lax

D = 3584
QHEADS = 28
KVH = 4
HEAD_DIM = 128
BLOCK = 128
TURN_MOST = 256
NDOC = 4
TOKENS = 8192
NBLOCKS = 64
TURNS = 64


def shared_keys(key):
    code_key = jax.random.fold_in(key, 11)
    scale_key = jax.random.fold_in(key, 12)
    codes = jnp.clip(jax.random.normal(code_key, (TOKENS, KVH * HEAD_DIM), jnp.float32), -4.0, 4.0)
    scales = jnp.exp(jax.random.uniform(scale_key, (2, TOKENS // BLOCK, KVH), jnp.float32, math.log(0.5), math.log(2.0)))
    return (codes, scales)


def draw_key_codes(key, part):
    return shared_keys(key)[0].astype(jnp.bfloat16)


def draw_kv_scales(key, part):
    return shared_keys(key)[1]


def draw_queries(key, part):
    base = jnp.clip(jax.random.normal(jax.random.fold_in(key, 21), (TOKENS, QHEADS * HEAD_DIM), jnp.float32), -4.0, 4.0)
    return base.astype(jnp.bfloat16)


def place_ends(entries, stream_key, smallest, largest):
    spot = [jax.random.randint(jax.random.fold_in(stream_key, axis), (), 0, length) for axis, length in enumerate(entries.shape)]
    main_axis = entries.shape.index(max(entries.shape))
    neighbour = spot[:main_axis] + [(spot[main_axis] + 1) % entries.shape[main_axis]] + spot[main_axis + 1:]
    return entries.at[tuple(spot)].set(smallest).at[tuple(neighbour)].set(largest)


def block_levels(stream_key, extent, shards, smallest, high):
    level = 1.0
    for dim, parts in shards:
        draws = jax.random.uniform(jax.random.fold_in(jax.random.fold_in(stream_key, 6), dim), (parts,), jnp.float32, smallest / len(shards), high / len(shards))
        level = level * jnp.repeat(jnp.exp(draws), extent[dim] // parts).reshape((-1,) + (1,) * (len(extent) - 1 - dim))
    return level


def profile(number_of, total, limit, slope):
    weights = [(1 << 20) // math.isqrt(rank ** slope) + 1 for rank in range(2, number_of + 1)]
    spare, counts = total - limit - (number_of - 1), [1] * (number_of - 1)
    while spare > 0:
        free = [i for i in range(number_of - 1) if counts[i] < limit]
        whole, remaining = sum([weights[i] for i in free]), spare
        for i in free:
            addition = min(limit - counts[i], max(1, remaining * weights[i] // whole), spare)
            counts[i] = counts[i] + addition
            spare = spare - addition
    return np.array([limit] + counts)


def ragged_sizes(key, amount, total, most, lean):
    if amount == 2:
        one = jax.random.randint(key, (), max(1, total - most), min(most, total - 1) + 1)
        return jnp.stack([one, total - one])
    tallies = jnp.asarray(profile(amount, total, most, lean), jnp.int32)
    couples = (amount - 1) // 2
    giver, sink = tallies[1:1 + 2 * couples:2], tallies[2:2 + 2 * couples:2]
    slack = jnp.minimum(giver - 1, most - sink)
    moved = jax.random.randint(jax.random.fold_in(key, 1), (couples,), 0, 1 << 20) % (slack + 1)
    tallies = tallies.at[1:1 + 2 * couples:2].set(giver - moved).at[2:2 + 2 * couples:2].set(sink + moved)
    return tallies[jax.random.permutation(jax.random.fold_in(key, 2), amount)]


def bell_draw(key, extent, scale, limit, shards=(), kind=jnp.bfloat16):
    values = scale * jax.random.normal(key, extent, jnp.float32)
    if shards:
        values = values * block_levels(key, extent, shards, -0.22, 0.18)
    return jnp.clip(values, -limit, limit).astype(kind)


def setup_inputs(seed: int = 0) -> dict:
    arg_keys = jax.random.split(jax.random.key(seed), 9)
    queries = draw_queries(jax.random.fold_in(arg_keys[8], 71), 0)
    key_codes = draw_key_codes(jax.random.fold_in(arg_keys[8], 71), 0)
    value_codes = bell_draw(arg_keys[2], (TOKENS, KVH * HEAD_DIM), 1.0, 4.0, ((0, 64), (1, 4)))
    kv_scales = draw_kv_scales(jax.random.fold_in(arg_keys[8], 71), 0)
    out_weight = bell_draw(arg_keys[4], (QHEADS * HEAD_DIM, D), (QHEADS * HEAD_DIM) ** -0.5, 0.09375, ((0, 4),))
    turn_ids = jnp.searchsorted(jnp.cumsum(ragged_sizes(arg_keys[5], TURNS, TOKENS, TURN_MOST, 1)), jnp.arange(TOKENS), side="right").astype(jnp.int32)
    block_mask = place_ends((jax.random.randint(arg_keys[6], (NBLOCKS, NBLOCKS), 0, 100) < 3).astype(jnp.int32), jax.random.fold_in(arg_keys[6], 1), 0, 1)
    doc_lengths = ragged_sizes(arg_keys[7], NDOC, TOKENS, TOKENS // 2, 1).astype(jnp.int32)
    return dict(queries=queries, key_codes=key_codes, value_codes=value_codes, kv_scales=kv_scales, out_weight=out_weight, turn_ids=turn_ids, block_mask=block_mask, doc_lengths=doc_lengths)


masked_score = -1e+30

def document_of(places, doc_lengths):
    ends = jnp.cumsum(doc_lengths)
    return lax.optimization_barrier(jnp.sum((places[:, None] >= ends[None, :]).astype(jnp.int32), axis=1))

def reference(queries, key_codes, value_codes, kv_scales, out_weight, turn_ids, block_mask, doc_lengths):
    groups = QHEADS // KVH
    key_scale = jnp.repeat(kv_scales[0], BLOCK, axis=0)
    value_scale = jnp.repeat(kv_scales[1], BLOCK, axis=0)
    keys = (key_codes.astype(jnp.float32).reshape(TOKENS, KVH, HEAD_DIM) * key_scale[:, :, None]).astype(jnp.bfloat16)
    values = (value_codes.astype(jnp.float32).reshape(TOKENS, KVH, HEAD_DIM) * value_scale[:, :, None]).astype(jnp.bfloat16)
    keys = lax.optimization_barrier(keys).astype(jnp.float32)
    values = lax.optimization_barrier(values).astype(jnp.float32)
    places = jnp.arange(TOKENS, dtype=jnp.int32)
    docs = document_of(places, doc_lengths)
    scaling = 1.0 / math.sqrt(HEAD_DIM)
    query_blocks = queries.reshape(NBLOCKS, BLOCK, KVH, groups, HEAD_DIM)

    def one_block(inputs):
        block_rows, index = inputs
        query_places = index * BLOCK + jnp.arange(BLOCK, dtype=jnp.int32)
        query_docs = lax.dynamic_slice_in_dim(docs, index * BLOCK, BLOCK)
        query_turns = lax.dynamic_slice_in_dim(turn_ids, index * BLOCK, BLOCK)
        mask_row = lax.dynamic_slice_in_dim(block_mask, index, 1, 0)[0]
        kept = jnp.repeat(mask_row, BLOCK) > 0
        same_block = places // BLOCK == index
        allowed = (places[None, :] <= query_places[:, None]) & (query_docs[:, None] == docs[None, :]) & ((query_turns[:, None] == turn_ids[None, :]) | kept[None, :] | same_block[None, :])
        scores = jnp.einsum('qhgd,khd->hgqk', block_rows.astype(jnp.float32), keys) * scaling
        scores = jnp.where(allowed[None, None], scores, masked_score)
        best = lax.optimization_barrier(jnp.max(scores, axis=3, keepdims=True))
        weights = jnp.where(allowed[None, None], jnp.exp(scores - best), 0.0)
        totals = lax.optimization_barrier(jnp.sum(weights, axis=3))
        rounded = lax.optimization_barrier(weights.astype(jnp.bfloat16)).astype(jnp.float32)
        summed = jnp.einsum('hgqk,khd->qhgd', rounded, values)
        result = summed / jnp.transpose(totals, (2, 0, 1))[:, :, :, None]
        return result.astype(jnp.bfloat16).reshape(BLOCK, QHEADS * HEAD_DIM)
    attended = lax.map(one_block, (query_blocks, jnp.arange(NBLOCKS, dtype=jnp.int32)))
    attended = attended.reshape(TOKENS, QHEADS * HEAD_DIM)
    return jnp.dot(attended, out_weight, preferred_element_type=jnp.float32).astype(jnp.bfloat16)
```

```python
import functools
import math

import jax
import jax.numpy as jnp
from jax import lax
from jax.experimental import pallas as pl
from jax.experimental.pallas import tpu as pltpu
from jax.sharding import PartitionSpec as P

HEAD_DIM = 128
BLOCK = 128
GROUPS = 7
WIDTH = GROUPS * HEAD_DIM
NX, NZ, NY = 2, 8, 4
NHEAD = 4
MASKED = -1e30
FACTOR = math.log2(math.e) / math.sqrt(HEAD_DIM)
MESH = pl.DeviceIdType.MESH
UP, DOWN = 0, 1
COLUMNS = ((0, 256), (256, 256), (512, 256), (768, 128))
CHUNKS = ((0, 512), (512, 384))


def kernel(
    q_ref,
    kc_ref,
    vc_ref,
    scale_ref,
    w_ref,
    turn_ref,
    mask_ref,
    doc_ref,
    out_ref,
    kv,
    qt,
    w,
    bias,
    best,
    totals,
    summed,
    attended,
    rs_out,
    rs_in,
    cross_out,
    cross_in,
    w_sem,
    send_z,
    recv_z,
    send_y,
    recv_y,
    send_relay,
    recv_relay,
    rs_send,
    rs_recv,
    cross_send,
    cross_recv,
):
    seq = lax.axis_index("seq")
    head = lax.axis_index("head")
    xh = seq // (NZ * NY)
    z = (seq // NY) % NZ
    y = seq % NY

    def at(to_xh, to_z, to_y):
        return (to_xh * (NZ * NY) + to_z * NY + to_y, head)

    left = at(xh, z, (y + NY - 1) % NY)
    right = at(xh, z, (y + 1) % NY)
    above = at(xh, (z + 1) % NZ, y)
    below = at(xh, (z + NZ - 1) % NZ, y)
    other = at(1 - xh, z, y)
    chip = head // 2
    core = head % 2
    sibling = (seq, chip * 2 + 1 - core)
    across = (seq, (1 - chip) * 2 + core)

    barrier = pltpu.get_barrier_semaphore()
    partners = (left, right, above, below, other, sibling, across)
    for partner in partners:
        pl.semaphore_signal(barrier, inc=1, device_id=partner, device_id_type=MESH)

    def weight_copy(part):
        return pltpu.make_async_copy(
            w_ref.at[:, pl.ds(part * WIDTH, WIDTH)], w.at[part], w_sem.at[part]
        )

    for part in range(NHEAD):
        weight_copy(part).start()

    kv[UP, z, y, 0] = (kc_ref[...].astype(jnp.float32) * scale_ref[0]).astype(jnp.bfloat16)
    kv[UP, z, y, 1] = jnp.transpose(vc_ref[...].astype(jnp.float32) * scale_ref[1]).astype(
        jnp.bfloat16
    )
    pl.semaphore_wait(barrier, len(partners))

    def z_copy(stream, row, target, slot_row):
        return pltpu.make_async_remote_copy(
            src_ref=kv.at[stream, row, y],
            dst_ref=kv.at[stream, row, y],
            send_sem=send_z.at[stream, slot_row],
            recv_sem=recv_z.at[stream, slot_row],
            device_id=target,
            device_id_type=MESH,
        )

    def x_copy():
        return pltpu.make_async_remote_copy(
            src_ref=kv.at[UP, z, y],
            dst_ref=kv.at[DOWN, z, y],
            send_sem=send_z.at[DOWN, z],
            recv_sem=recv_z.at[DOWN, z],
            device_id=other,
            device_id_type=MESH,
        )

    def y_copy(stream, row, column, target, side):
        return pltpu.make_async_remote_copy(
            src_ref=kv.at[stream, row, column],
            dst_ref=kv.at[stream, row, column],
            send_sem=send_y.at[stream, row, side],
            recv_sem=recv_y.at[stream, row, side],
            device_id=target,
            device_id_type=MESH,
        )

    def relay_copy(stream, row, column, half, target):
        return pltpu.make_async_remote_copy(
            src_ref=kv.at[stream, row, column, half],
            dst_ref=kv.at[stream, row, column, half],
            send_sem=send_relay.at[stream, row, half],
            recv_sem=recv_relay.at[stream, row, half],
            device_id=target,
            device_id_type=MESH,
        )

    y_left = (y + NY - 1) % NY
    y_right = (y + 1) % NY
    y_far = (y + 2) % NY

    @pl.when(xh == 0)
    def _():
        x_copy().start()

    def active(stream, step):
        if stream == UP:
            return (step >= 0) & (step <= z), z - step, above, z < NZ - 1
        return (xh == 1) & (step >= 0) & (step <= NZ - 1 - z), z + step, below, z > 0

    def forward(stream, step):
        on, row, target, more = active(stream, step)

        @pl.when(on)
        def _():
            if stream == UP:

                @pl.when(step > 0)
                def _():
                    z_copy(stream, row, target, row).wait_recv()
            else:
                z_copy(stream, row, target, row).wait_recv()

            @pl.when(more)
            def _():
                z_copy(stream, row, target, row).start()

            y_copy(stream, row, y, right, 0).start()
            y_copy(stream, row, y, left, 1).start()

    def relay(stream, step):
        on, row, _, _ = active(stream, step)

        @pl.when(on)
        def _():
            y_copy(stream, row, y_left, right, 0).wait_recv()
            relay_copy(stream, row, y_left, 0, right).start()
            y_copy(stream, row, y_right, left, 1).wait_recv()
            relay_copy(stream, row, y_right, 1, left).start()

    def drain(stream, step):
        on, row, target, more = active(stream, step)

        @pl.when(on)
        def _():
            @pl.when(more)
            def _():
                z_copy(stream, row, target, row).wait_send()

            y_copy(stream, row, y, right, 0).wait_send()
            y_copy(stream, row, y, left, 1).wait_send()
            relay_copy(stream, row, y_left, 0, right).wait_send()
            relay_copy(stream, row, y_right, 1, left).wait_send()

    lanes = lax.broadcasted_iota(jnp.int32, (1, BLOCK), 1)
    places = seq * BLOCK + lanes
    doc_start = jnp.zeros((1, BLOCK), jnp.int32)
    end = doc_ref[0]
    for index in range(doc_ref.shape[0]):
        doc_start = jnp.where(places >= end, end, doc_start)
        if index + 1 < doc_ref.shape[0]:
            end = end + doc_ref[index + 1]
    own_turns = turn_ref[pl.ds(seq, 1), :]
    earlier = jnp.zeros((1, BLOCK), jnp.int32)
    for back in range(3):
        block = jnp.maximum(seq - back, 0)
        row = turn_ref[pl.ds(block, 1), :].astype(jnp.float32)
        column = jnp.transpose(jnp.broadcast_to(row, (BLOCK, BLOCK))).astype(jnp.int32)
        count = jnp.sum(jnp.where(column < own_turns, 1, 0), axis=0, keepdims=True)
        earlier = earlier + jnp.where(seq >= back, count, 0)
    turn_start = jnp.maximum(seq - 2, 0) * BLOCK + earlier
    key_rows = lax.broadcasted_iota(jnp.int32, (BLOCK, BLOCK), 0)

    for group in range(GROUPS):
        part = slice(group * HEAD_DIM, (group + 1) * HEAD_DIM)
        qt[:, part] = jnp.transpose(q_ref[:, part].astype(jnp.float32)).astype(jnp.bfloat16)
    best[...] = jnp.full_like(best, MASKED)
    totals[...] = jnp.zeros_like(totals)
    summed[...] = jnp.zeros_like(summed)

    def attend(stream, step):
        on, row, _, _ = active(stream, step)

        @pl.when(on)
        def _():
            relay_copy(stream, row, y_far, 0, right).wait_recv()
            relay_copy(stream, row, y_far, 1, left).wait_recv()
            first = row * NY + (xh * (NZ * NY) if stream == UP else 0)
            for column in range(NY):
                block = first + column
                kept = (mask_ref[0, block] == 1) | (block == seq)
                low = jnp.maximum(doc_start, jnp.where(kept, 0, turn_start)) - block * BLOCK
                high = places - block * BLOCK
                allowed = (key_rows >= low) & (key_rows <= high)
                tile = jnp.where(allowed, 0.0, MASKED)
                bias[pl.ds(column * BLOCK, BLOCK), pl.ds(0, BLOCK)] = tile
                bias[pl.ds(column * BLOCK, BLOCK), pl.ds(BLOCK, BLOCK)] = tile
            keys = jnp.concatenate([kv[stream, row, c, 0] for c in range(NY)], axis=0)
            values = jnp.concatenate([kv[stream, row, c, 1] for c in range(NY)], axis=1)
            for start, width in COLUMNS:
                part = pl.ds(start, width)
                scores = (
                    jnp.dot(keys, qt[:, part], preferred_element_type=jnp.float32)
                    + bias[:, pl.ds(0, width)]
                )
                previous = best[:, part]
                newest = jnp.maximum(previous, jnp.max(scores, axis=0, keepdims=True))
                factor = jnp.exp2((previous - newest) * FACTOR)
                weights = jnp.exp2((scores - newest) * FACTOR)
                best[:, part] = newest
                totals[:, part] = totals[:, part] * factor + jnp.sum(
                    weights, axis=0, keepdims=True
                )
                summed[:, part] = summed[:, part] * factor + jnp.dot(
                    values, weights.astype(jnp.bfloat16), preferred_element_type=jnp.float32
                )

    def advance(step, carry):
        forward(UP, step)
        forward(DOWN, step)
        relay(UP, step - 1)
        relay(DOWN, step - 1)
        attend(UP, step - 2)
        attend(DOWN, step - 2)
        return carry

    lax.fori_loop(0, NZ + 2, advance, 0)

    for group in range(GROUPS):
        part = slice(group * HEAD_DIM, (group + 1) * HEAD_DIM)
        attended[:, part] = jnp.transpose(summed[:, part] / totals[:, part]).astype(jnp.bfloat16)
    for part in range(NHEAD):
        weight_copy(part).wait()

    def project(part, start, width):
        return jnp.dot(
            attended[...],
            w[part, :, pl.ds(start, width)],
            preferred_element_type=jnp.float32,
        )

    def sibling_copy(index):
        start, width = CHUNKS[index % 2]
        place = index // 2
        return pltpu.make_async_remote_copy(
            src_ref=rs_out.at[place, :, pl.ds(start, width)],
            dst_ref=rs_in.at[place, :, pl.ds(start, width)],
            send_sem=rs_send.at[index],
            recv_sem=rs_recv.at[index],
            device_id=sibling,
            device_id_type=MESH,
        )

    def cross_copy(index):
        start, width = CHUNKS[index]
        return pltpu.make_async_remote_copy(
            src_ref=cross_out.at[:, pl.ds(start, width)],
            dst_ref=cross_in.at[:, pl.ds(start, width)],
            send_sem=cross_send.at[index],
            recv_sem=cross_recv.at[index],
            device_id=across,
            device_id_type=MESH,
        )

    far = 1 - chip
    for index, (start, width) in enumerate(CHUNKS):
        rs_out[0, :, pl.ds(start, width)] = project(far * 2 + 1 - core, start, width).astype(
            jnp.bfloat16
        )
        sibling_copy(index).start()
    for index, (start, width) in enumerate(CHUNKS):
        mine = project(far * 2 + core, start, width)
        sibling_copy(index).wait_recv()
        cross_out[:, pl.ds(start, width)] = (
            mine + rs_in[0, :, pl.ds(start, width)].astype(jnp.float32)
        ).astype(jnp.bfloat16)
        cross_copy(index).start()
    for index, (start, width) in enumerate(CHUNKS):
        rs_out[1, :, pl.ds(start, width)] = project(chip * 2 + 1 - core, start, width).astype(
            jnp.bfloat16
        )
        sibling_copy(2 + index).start()
    for index, (start, width) in enumerate(CHUNKS):
        mine = project(head, start, width)
        sibling_copy(2 + index).wait_recv()
        mine = mine + rs_in[1, :, pl.ds(start, width)].astype(jnp.float32)
        cross_copy(index).wait_recv()
        out_ref[:, pl.ds(start, width)] = (
            mine + cross_in[:, pl.ds(start, width)].astype(jnp.float32)
        ).astype(jnp.bfloat16)

    for index in range(4):
        sibling_copy(index).wait_send()
    for index in range(2):
        cross_copy(index).wait_send()

    @pl.when(xh == 0)
    def _():
        x_copy().wait_send()

    def finish(step, carry):
        drain(UP, step)
        drain(DOWN, step)
        return carry

    lax.fori_loop(0, NZ, finish, 0)


def on_device(
    queries, key_codes, value_codes, kv_scales, out_weight, turn_ids, block_mask, doc_lengths
):
    vmem = pl.BlockSpec(memory_space=pltpu.VMEM)
    smem = pl.BlockSpec(memory_space=pltpu.SMEM)
    dma = pltpu.SemaphoreType.DMA
    return pl.pallas_call(
        kernel,
        out_shape=jax.ShapeDtypeStruct(queries.shape, jnp.bfloat16),
        in_specs=[
            vmem,
            vmem,
            vmem,
            smem,
            pl.BlockSpec(memory_space=pl.ANY),
            vmem,
            smem,
            smem,
        ],
        out_specs=vmem,
        scratch_shapes=[
            pltpu.VMEM((2, NZ, NY, 2, BLOCK, HEAD_DIM), jnp.bfloat16),
            pltpu.VMEM((HEAD_DIM, WIDTH), jnp.bfloat16),
            pltpu.VMEM((NHEAD, WIDTH, WIDTH), jnp.bfloat16),
            pltpu.VMEM((NY * BLOCK, 2 * BLOCK), jnp.float32),
            pltpu.VMEM((1, WIDTH), jnp.float32),
            pltpu.VMEM((1, WIDTH), jnp.float32),
            pltpu.VMEM((HEAD_DIM, WIDTH), jnp.float32),
            pltpu.VMEM((BLOCK, WIDTH), jnp.bfloat16),
            pltpu.VMEM((2, BLOCK, WIDTH), jnp.bfloat16),
            pltpu.VMEM((2, BLOCK, WIDTH), jnp.bfloat16),
            pltpu.VMEM((BLOCK, WIDTH), jnp.bfloat16),
            pltpu.VMEM((BLOCK, WIDTH), jnp.bfloat16),
            dma((NHEAD,)),
            dma((2, NZ)),
            dma((2, NZ)),
            dma((2, NZ, 2)),
            dma((2, NZ, 2)),
            dma((2, NZ, 2)),
            dma((2, NZ, 2)),
            dma((4,)),
            dma((4,)),
            dma((2,)),
            dma((2,)),
        ],
        compiler_params=pltpu.CompilerParams(
            collective_id=0, has_side_effects=True, vmem_limit_bytes=40 * 1024 * 1024
        ),
    )(
        queries,
        key_codes,
        value_codes,
        kv_scales.reshape(2),
        out_weight,
        turn_ids.reshape(-1, BLOCK),
        block_mask,
        doc_lengths,
    )


def solution(mesh):
    placed = (
        P("seq", "head"),
        P("seq", "head"),
        P("seq", "head"),
        P(None, "seq", "head"),
        P("head", None),
        P(),
        P("seq", None),
        P(),
    )
    return jax.shard_map(
        on_device, mesh=mesh, in_specs=placed, out_specs=P("seq", "head"), check_vma=False
    )
```

```python
import functools
import math

import jax
import jax.numpy as jnp
from jax import lax
from jax.experimental import pallas as pl
from jax.experimental.pallas import tpu as pltpu
from jax.sharding import PartitionSpec as P

HEAD_DIM = 128
BLOCK = 128
GROUPS = 7
WIDTH = GROUPS * HEAD_DIM
NX, NZ, NY = 2, 8, 4
NHEAD = 4
MASKED = -1e30
FACTOR = math.log2(math.e) / math.sqrt(HEAD_DIM)
MESH = pl.DeviceIdType.MESH
UP, DOWN = 0, 1
WINDOW, RELAY_LAG, ATTEND_LAG = 3, 2, 4
COLUMNS = ((0, 256), (256, 256), (512, 256), (768, 128))
CHUNKS = ((0, 512), (512, 384))


def kernel(
    q_hbm,
    kc_hbm,
    vc_hbm,
    scale_hbm,
    w_ref,
    turn_hbm,
    mask_hbm,
    doc_hbm,
    out_ref,
    q_ref,
    kc_ref,
    vc_ref,
    scale_ref,
    turn_ref,
    mask_ref,
    doc_ref,
    kv,
    qt,
    w,
    bias,
    best,
    totals,
    summed,
    attended,
    rs_out,
    rs_in,
    cross_out,
    cross_in,
    w_sem,
    in_sem,
    send_z,
    recv_z,
    send_y,
    recv_y,
    send_relay,
    recv_relay,
    rs_send,
    rs_recv,
    cross_send,
    cross_recv,
):
    seq = lax.axis_index("seq")
    head = lax.axis_index("head")
    xh = seq // (NZ * NY)
    z = (seq // NY) % NZ
    y = seq % NY

    def at(to_xh, to_z, to_y):
        return (to_xh * (NZ * NY) + to_z * NY + to_y, head)

    left = at(xh, z, (y + NY - 1) % NY)
    right = at(xh, z, (y + 1) % NY)
    other = at(1 - xh, z, y)
    chip = head // 2
    core = head % 2
    sibling = (seq, chip * 2 + 1 - core)
    across = (seq, (1 - chip) * 2 + core)

    barrier = pltpu.get_barrier_semaphore()
    partners = [left, right, sibling, across, other]
    for step in range(1, NZ):
        partners += [at(xh, (z + step) % NZ, y), at(1 - xh, (z + step) % NZ, y)]
    for partner in partners:
        pl.semaphore_signal(barrier, inc=1, device_id=partner, device_id_type=MESH)

    def weight_copy(part):
        return pltpu.make_async_copy(
            w_ref.at[:, pl.ds(part * WIDTH, WIDTH)], w.at[part], w_sem.at[part]
        )

    staged = (
        (kc_hbm, kc_ref),
        (vc_hbm, vc_ref),
        (scale_hbm, scale_ref),
        (doc_hbm, doc_ref),
        (turn_hbm, turn_ref),
        (mask_hbm, mask_ref),
        (q_hbm, q_ref),
    )
    stage = [
        pltpu.make_async_copy(source, target, in_sem.at[index])
        for index, (source, target) in enumerate(staged)
    ]
    for copy in stage:
        copy.start()
    for copy in stage[:3]:
        copy.wait()

    kv[UP, z, y, 0] = (kc_ref[...].astype(jnp.float32) * scale_ref[0]).astype(jnp.bfloat16)
    kv[UP, z, y, 1] = jnp.transpose(vc_ref[...].astype(jnp.float32) * scale_ref[1]).astype(
        jnp.bfloat16
    )
    pl.semaphore_wait(barrier, len(partners))

    def up_copy(step):
        return pltpu.make_async_remote_copy(
            src_ref=kv.at[UP, z, y],
            dst_ref=kv.at[UP, z, y],
            send_sem=send_z.at[UP, step],
            recv_sem=recv_z.at[UP, z],
            device_id=at(xh, (z + step) % NZ, y),
            device_id_type=MESH,
        )

    def down_copy(step):
        return pltpu.make_async_remote_copy(
            src_ref=kv.at[UP, z, y],
            dst_ref=kv.at[DOWN, z, y],
            send_sem=send_z.at[DOWN, step],
            recv_sem=recv_z.at[DOWN, z],
            device_id=at(1 - xh, (z + NZ - step) % NZ, y),
            device_id_type=MESH,
        )

    def arrival(stream, row):
        return pltpu.make_async_remote_copy(
            src_ref=kv.at[stream, row, y],
            dst_ref=kv.at[stream, row, y],
            send_sem=send_z.at[stream, 0],
            recv_sem=recv_z.at[stream, row],
            device_id=other,
            device_id_type=MESH,
        )

    def y_copy(stream, row, column, target, side):
        return pltpu.make_async_remote_copy(
            src_ref=kv.at[stream, row, column],
            dst_ref=kv.at[stream, row, column],
            send_sem=send_y.at[stream, row, side],
            recv_sem=recv_y.at[stream, row, side],
            device_id=target,
            device_id_type=MESH,
        )

    def relay_copy(stream, row, column, half, target):
        return pltpu.make_async_remote_copy(
            src_ref=kv.at[stream, row, column, half],
            dst_ref=kv.at[stream, row, column, half],
            send_sem=send_relay.at[stream, row, half],
            recv_sem=recv_relay.at[stream, row, half],
            device_id=target,
            device_id_type=MESH,
        )

    y_left = (y + NY - 1) % NY
    y_right = (y + 1) % NY
    y_far = (y + 2) % NY

    def active(stream, step):
        if stream == UP:
            return (step >= 0) & (step <= z), z - step
        return (xh == 1) & (step >= 0) & (step <= NZ - 1 - z), z + step

    def column_send(step, act):
        @pl.when((xh == 0) & (step <= z))
        def _():
            act(down_copy(step))

        @pl.when((step > 0) & (z + step < NZ))
        def _():
            act(up_copy(step))

    def forward(stream, step):
        on, row = active(stream, step)

        if stream == UP:
            on = on & (step > 0)

        @pl.when(on)
        def _():
            arrival(stream, row).wait_recv()
            y_copy(stream, row, y, right, 0).start()
            y_copy(stream, row, y, left, 1).start()

    y_copy(UP, z, y, right, 0).start()
    y_copy(UP, z, y, left, 1).start()
    for step in range(WINDOW):
        column_send(step, lambda copy: copy.start())
    for part in range(NHEAD):
        weight_copy(part).start()

    def relay(stream, step):
        on, row = active(stream, step)

        @pl.when(on)
        def _():
            y_copy(stream, row, y_left, right, 0).wait_recv()
            relay_copy(stream, row, y_left, 0, right).start()
            y_copy(stream, row, y_right, left, 1).wait_recv()
            relay_copy(stream, row, y_right, 1, left).start()

    def drain(stream, step):
        on, row = active(stream, step)

        @pl.when(on)
        def _():
            y_copy(stream, row, y, right, 0).wait_send()
            y_copy(stream, row, y, left, 1).wait_send()
            relay_copy(stream, row, y_left, 0, right).wait_send()
            relay_copy(stream, row, y_right, 1, left).wait_send()

    for copy in stage[3:]:
        copy.wait()

    lanes = lax.broadcasted_iota(jnp.int32, (1, BLOCK), 1)
    places = seq * BLOCK + lanes
    doc_start = jnp.zeros((1, BLOCK), jnp.int32)
    end = doc_ref[0]
    for index in range(doc_ref.shape[0]):
        doc_start = jnp.where(places >= end, end, doc_start)
        if index + 1 < doc_ref.shape[0]:
            end = end + doc_ref[index + 1]
    own_turns = turn_ref[pl.ds(seq, 1), :]
    earlier = jnp.zeros((1, BLOCK), jnp.int32)
    for back in range(3):
        block = jnp.maximum(seq - back, 0)
        row = turn_ref[pl.ds(block, 1), :].astype(jnp.float32)
        column = jnp.transpose(jnp.broadcast_to(row, (BLOCK, BLOCK))).astype(jnp.int32)
        count = jnp.sum(jnp.where(column < own_turns, 1, 0), axis=0, keepdims=True)
        earlier = earlier + jnp.where(seq >= back, count, 0)
    turn_start = jnp.maximum(seq - 2, 0) * BLOCK + earlier
    key_rows = lax.broadcasted_iota(jnp.int32, (BLOCK, BLOCK), 0)

    for group in range(GROUPS):
        part = slice(group * HEAD_DIM, (group + 1) * HEAD_DIM)
        qt[:, part] = jnp.transpose(q_ref[:, part].astype(jnp.float32)).astype(jnp.bfloat16)
    best[...] = jnp.full_like(best, MASKED)
    totals[...] = jnp.zeros_like(totals)
    summed[...] = jnp.zeros_like(summed)

    def attend(stream, step):
        on, row = active(stream, step)

        @pl.when(on)
        def _():
            relay_copy(stream, row, y_far, 0, right).wait_recv()
            relay_copy(stream, row, y_far, 1, left).wait_recv()
            first = row * NY + (xh * (NZ * NY) if stream == UP else 0)
            for column in range(NY):
                block = first + column
                kept = (mask_ref[0, block] == 1) | (block == seq)
                low = jnp.maximum(doc_start, jnp.where(kept, 0, turn_start)) - block * BLOCK
                high = places - block * BLOCK
                allowed = (key_rows >= low) & (key_rows <= high)
                tile = jnp.where(allowed, 0.0, MASKED)
                bias[pl.ds(column * BLOCK, BLOCK), pl.ds(0, BLOCK)] = tile
                bias[pl.ds(column * BLOCK, BLOCK), pl.ds(BLOCK, BLOCK)] = tile
            keys = jnp.concatenate([kv[stream, row, c, 0] for c in range(NY)], axis=0)
            values = jnp.concatenate([kv[stream, row, c, 1] for c in range(NY)], axis=1)
            for start, width in COLUMNS:
                part = pl.ds(start, width)
                scores = (
                    jnp.dot(keys, qt[:, part], preferred_element_type=jnp.float32)
                    + bias[:, pl.ds(0, width)]
                )
                previous = best[:, part]
                newest = jnp.maximum(previous, jnp.max(scores, axis=0, keepdims=True))
                factor = jnp.exp2((previous - newest) * FACTOR)
                weights = jnp.exp2((scores - newest) * FACTOR)
                best[:, part] = newest
                totals[:, part] = totals[:, part] * factor + jnp.sum(
                    weights, axis=0, keepdims=True
                )
                summed[:, part] = summed[:, part] * factor + jnp.dot(
                    values, weights.astype(jnp.bfloat16), preferred_element_type=jnp.float32
                )

    def advance(step, carry):
        @pl.when(step < NZ)
        def _():
            forward(UP, step)
            forward(DOWN, step)
            column_send(step, lambda copy: copy.wait_send())

        column_send(step + WINDOW, lambda copy: copy.start())
        relay(UP, step - RELAY_LAG)
        relay(DOWN, step - RELAY_LAG)
        attend(UP, step - ATTEND_LAG)
        attend(DOWN, step - ATTEND_LAG)
        return carry

    lax.fori_loop(0, NZ + ATTEND_LAG, advance, 0)

    for group in range(GROUPS):
        part = slice(group * HEAD_DIM, (group + 1) * HEAD_DIM)
        attended[:, part] = jnp.transpose(summed[:, part] / totals[:, part]).astype(jnp.bfloat16)
    for part in range(NHEAD):
        weight_copy(part).wait()

    def project(part, start, width):
        return jnp.dot(
            attended[...],
            w[part, :, pl.ds(start, width)],
            preferred_element_type=jnp.float32,
        )

    def sibling_copy(index):
        start, width = CHUNKS[index % 2]
        place = index // 2
        return pltpu.make_async_remote_copy(
            src_ref=rs_out.at[place, :, pl.ds(start, width)],
            dst_ref=rs_in.at[place, :, pl.ds(start, width)],
            send_sem=rs_send.at[index],
            recv_sem=rs_recv.at[index],
            device_id=sibling,
            device_id_type=MESH,
        )

    def cross_copy(index):
        start, width = CHUNKS[index]
        return pltpu.make_async_remote_copy(
            src_ref=cross_out.at[:, pl.ds(start, width)],
            dst_ref=cross_in.at[:, pl.ds(start, width)],
            send_sem=cross_send.at[index],
            recv_sem=cross_recv.at[index],
            device_id=across,
            device_id_type=MESH,
        )

    far = 1 - chip
    for index, (start, width) in enumerate(CHUNKS):
        rs_out[0, :, pl.ds(start, width)] = project(far * 2 + 1 - core, start, width).astype(
            jnp.bfloat16
        )
        sibling_copy(index).start()
    for index, (start, width) in enumerate(CHUNKS):
        mine = project(far * 2 + core, start, width)
        sibling_copy(index).wait_recv()
        cross_out[:, pl.ds(start, width)] = (
            mine + rs_in[0, :, pl.ds(start, width)].astype(jnp.float32)
        ).astype(jnp.bfloat16)
        cross_copy(index).start()
    for index, (start, width) in enumerate(CHUNKS):
        rs_out[1, :, pl.ds(start, width)] = project(chip * 2 + 1 - core, start, width).astype(
            jnp.bfloat16
        )
        sibling_copy(2 + index).start()
    for index, (start, width) in enumerate(CHUNKS):
        mine = project(head, start, width)
        sibling_copy(2 + index).wait_recv()
        mine = mine + rs_in[1, :, pl.ds(start, width)].astype(jnp.float32)
        cross_copy(index).wait_recv()
        out_ref[:, pl.ds(start, width)] = (
            mine + cross_in[:, pl.ds(start, width)].astype(jnp.float32)
        ).astype(jnp.bfloat16)

    for index in range(4):
        sibling_copy(index).wait_send()
    for index in range(2):
        cross_copy(index).wait_send()

    def finish(step, carry):
        drain(UP, step)
        drain(DOWN, step)
        return carry

    lax.fori_loop(0, NZ, finish, 0)


def on_device(
    queries, key_codes, value_codes, kv_scales, out_weight, turn_ids, block_mask, doc_lengths
):
    dma = pltpu.SemaphoreType.DMA
    return pl.pallas_call(
        kernel,
        out_shape=jax.ShapeDtypeStruct(queries.shape, jnp.bfloat16),
        in_specs=[pl.BlockSpec(memory_space=pltpu.HBM)] * 8,
        out_specs=pl.BlockSpec(memory_space=pltpu.VMEM),
        scratch_shapes=[
            pltpu.VMEM(queries.shape, jnp.bfloat16),
            pltpu.VMEM(key_codes.shape, jnp.bfloat16),
            pltpu.VMEM(value_codes.shape, jnp.bfloat16),
            pltpu.SMEM((2,), jnp.float32),
            pltpu.VMEM((turn_ids.shape[0] // BLOCK, BLOCK), jnp.int32),
            pltpu.SMEM(block_mask.shape, jnp.int32),
            pltpu.SMEM(doc_lengths.shape, jnp.int32),
            pltpu.VMEM((2, NZ, NY, 2, BLOCK, HEAD_DIM), jnp.bfloat16),
            pltpu.VMEM((HEAD_DIM, WIDTH), jnp.bfloat16),
            pltpu.VMEM((NHEAD, WIDTH, WIDTH), jnp.bfloat16),
            pltpu.VMEM((NY * BLOCK, 2 * BLOCK), jnp.float32),
            pltpu.VMEM((1, WIDTH), jnp.float32),
            pltpu.VMEM((1, WIDTH), jnp.float32),
            pltpu.VMEM((HEAD_DIM, WIDTH), jnp.float32),
            pltpu.VMEM((BLOCK, WIDTH), jnp.bfloat16),
            pltpu.VMEM((2, BLOCK, WIDTH), jnp.bfloat16),
            pltpu.VMEM((2, BLOCK, WIDTH), jnp.bfloat16),
            pltpu.VMEM((BLOCK, WIDTH), jnp.bfloat16),
            pltpu.VMEM((BLOCK, WIDTH), jnp.bfloat16),
            dma((NHEAD,)),
            dma((7,)),
            dma((2, NZ)),
            dma((2, NZ)),
            dma((2, NZ, 2)),
            dma((2, NZ, 2)),
            dma((2, NZ, 2)),
            dma((2, NZ, 2)),
            dma((4,)),
            dma((4,)),
            dma((2,)),
            dma((2,)),
        ],
        compiler_params=pltpu.CompilerParams(
            collective_id=0, has_side_effects=True, vmem_limit_bytes=40 * 1024 * 1024
        ),
    )(
        *(
            pltpu.with_memory_space_constraint(operand, pltpu.HBM)
            for operand in (
                queries,
                key_codes,
                value_codes,
                kv_scales.reshape(2),
                out_weight,
                turn_ids.reshape(-1, BLOCK),
                block_mask,
                doc_lengths,
            )
        )
    )


def solution(mesh):
    placed = (
        P("seq", "head"),
        P("seq", "head"),
        P("seq", "head"),
        P(None, "seq", "head"),
        P("head", None),
        P(),
        P("seq", None),
        P(),
    )
    return jax.shard_map(
        on_device, mesh=mesh, in_specs=placed, out_specs=P("seq", "head"), check_vma=False
    )
```

```python
import functools
import math

import jax
import jax.numpy as jnp
from jax import lax
from jax.experimental import pallas as pl
from jax.experimental.pallas import tpu as pltpu
from jax.sharding import PartitionSpec as P

HEAD_DIM = 128
BLOCK = 128
GROUPS = 7
WIDTH = GROUPS * HEAD_DIM
NX, NZ, NY = 2, 8, 4
NHEAD = 4
MASKED = -1e30
FACTOR = math.log2(math.e) / math.sqrt(HEAD_DIM)
MESH = pl.DeviceIdType.MESH
UP, DOWN = 0, 1
WINDOW, RELAY_LAG, ATTEND_LAG = 3, 2, 4
HEADS = 2
CHUNKS = ((0, 512), (512, 384))


def kernel(
    q_hbm,
    kc_hbm,
    vc_hbm,
    scale_hbm,
    w_ref,
    turn_hbm,
    mask_hbm,
    doc_hbm,
    out_ref,
    q_ref,
    kc_ref,
    vc_ref,
    scale_ref,
    turn_ref,
    mask_ref,
    doc_ref,
    kv,
    q_rows,
    w,
    bias,
    starts,
    best,
    summed,
    attended,
    rs_out,
    rs_in,
    cross_out,
    cross_in,
    w_sem,
    in_sem,
    send_z,
    recv_z,
    send_y,
    recv_y,
    send_relay,
    recv_relay,
    rs_send,
    rs_recv,
    cross_send,
    cross_recv,
):
    seq = lax.axis_index("seq")
    head = lax.axis_index("head")
    xh = seq // (NZ * NY)
    z = (seq // NY) % NZ
    y = seq % NY

    def at(to_xh, to_z, to_y):
        return (to_xh * (NZ * NY) + to_z * NY + to_y, head)

    left = at(xh, z, (y + NY - 1) % NY)
    right = at(xh, z, (y + 1) % NY)
    other = at(1 - xh, z, y)
    chip = head // 2
    core = head % 2
    sibling = (seq, chip * 2 + 1 - core)
    across = (seq, (1 - chip) * 2 + core)

    barrier = pltpu.get_barrier_semaphore()
    partners = [left, right, sibling, across, other]
    for step in range(1, NZ):
        partners += [at(xh, (z + step) % NZ, y), at(1 - xh, (z + step) % NZ, y)]
    for partner in partners:
        pl.semaphore_signal(barrier, inc=1, device_id=partner, device_id_type=MESH)

    def weight_copy(part):
        return pltpu.make_async_copy(
            w_ref.at[:, pl.ds(part * WIDTH, WIDTH)], w.at[part], w_sem.at[part]
        )

    staged = (
        (kc_hbm, kc_ref),
        (vc_hbm, vc_ref),
        (scale_hbm, scale_ref),
        (doc_hbm, doc_ref),
        (turn_hbm, turn_ref),
        (mask_hbm, mask_ref),
        (q_hbm, q_ref),
    )
    stage = [
        pltpu.make_async_copy(source, target, in_sem.at[index])
        for index, (source, target) in enumerate(staged)
    ]
    for copy in stage:
        copy.start()
    for copy in stage[:3]:
        copy.wait()

    kv[UP, z, y, 0] = (kc_ref[...].astype(jnp.float32) * scale_ref[0]).astype(jnp.bfloat16)
    kv[UP, z, y, 1] = (vc_ref[...].astype(jnp.float32) * scale_ref[1]).astype(jnp.bfloat16)
    pl.semaphore_wait(barrier, len(partners))

    def up_copy(step):
        return pltpu.make_async_remote_copy(
            src_ref=kv.at[UP, z, y],
            dst_ref=kv.at[UP, z, y],
            send_sem=send_z.at[UP, step],
            recv_sem=recv_z.at[UP, z],
            device_id=at(xh, (z + step) % NZ, y),
            device_id_type=MESH,
        )

    def down_copy(step):
        return pltpu.make_async_remote_copy(
            src_ref=kv.at[UP, z, y],
            dst_ref=kv.at[DOWN, z, y],
            send_sem=send_z.at[DOWN, step],
            recv_sem=recv_z.at[DOWN, z],
            device_id=at(1 - xh, (z + NZ - step) % NZ, y),
            device_id_type=MESH,
        )

    def arrival(stream, row):
        return pltpu.make_async_remote_copy(
            src_ref=kv.at[stream, row, y],
            dst_ref=kv.at[stream, row, y],
            send_sem=send_z.at[stream, 0],
            recv_sem=recv_z.at[stream, row],
            device_id=other,
            device_id_type=MESH,
        )

    def y_copy(stream, row, column, target, side):
        return pltpu.make_async_remote_copy(
            src_ref=kv.at[stream, row, column],
            dst_ref=kv.at[stream, row, column],
            send_sem=send_y.at[stream, row, side],
            recv_sem=recv_y.at[stream, row, side],
            device_id=target,
            device_id_type=MESH,
        )

    def relay_copy(stream, row, column, half, target):
        return pltpu.make_async_remote_copy(
            src_ref=kv.at[stream, row, column, half],
            dst_ref=kv.at[stream, row, column, half],
            send_sem=send_relay.at[stream, row, half],
            recv_sem=recv_relay.at[stream, row, half],
            device_id=target,
            device_id_type=MESH,
        )

    y_left = (y + NY - 1) % NY
    y_right = (y + 1) % NY
    y_far = (y + 2) % NY

    def active(stream, step):
        if stream == UP:
            return (step >= 0) & (step <= z), z - step
        return (xh == 1) & (step >= 0) & (step <= NZ - 1 - z), z + step

    def column_send(step, act):
        @pl.when((xh == 0) & (step <= z))
        def _():
            act(down_copy(step))

        @pl.when((step > 0) & (z + step < NZ))
        def _():
            act(up_copy(step))

    def forward(stream, step):
        on, row = active(stream, step)

        if stream == UP:
            on = on & (step > 0)

        @pl.when(on)
        def _():
            arrival(stream, row).wait_recv()
            y_copy(stream, row, y, right, 0).start()
            y_copy(stream, row, y, left, 1).start()

    y_copy(UP, z, y, right, 0).start()
    y_copy(UP, z, y, left, 1).start()
    for step in range(WINDOW):
        column_send(step, lambda copy: copy.start())
    for part in range(NHEAD):
        weight_copy(part).start()

    def relay(stream, step):
        on, row = active(stream, step)

        @pl.when(on)
        def _():
            y_copy(stream, row, y_left, right, 0).wait_recv()
            relay_copy(stream, row, y_left, 0, right).start()
            y_copy(stream, row, y_right, left, 1).wait_recv()
            relay_copy(stream, row, y_right, 1, left).start()

    def drain(stream, step):
        on, row = active(stream, step)

        @pl.when(on)
        def _():
            y_copy(stream, row, y, right, 0).wait_send()
            y_copy(stream, row, y, left, 1).wait_send()
            relay_copy(stream, row, y_left, 0, right).wait_send()
            relay_copy(stream, row, y_right, 1, left).wait_send()

    for copy in stage[3:]:
        copy.wait()

    lanes = lax.broadcasted_iota(jnp.int32, (1, BLOCK), 1)
    places = seq * BLOCK + lanes
    doc_start = jnp.zeros((1, BLOCK), jnp.int32)
    end = doc_ref[0]
    for index in range(doc_ref.shape[0]):
        doc_start = jnp.where(places >= end, end, doc_start)
        if index + 1 < doc_ref.shape[0]:
            end = end + doc_ref[index + 1]
    own_turns = turn_ref[pl.ds(seq, 1), :]
    earlier = jnp.zeros((1, BLOCK), jnp.int32)
    for back in range(3):
        block = jnp.maximum(seq - back, 0)
        row = turn_ref[pl.ds(block, 1), :].astype(jnp.float32)
        column = jnp.transpose(jnp.broadcast_to(row, (BLOCK, BLOCK))).astype(jnp.int32)
        count = jnp.sum(jnp.where(column < own_turns, 1, 0), axis=0, keepdims=True)
        earlier = earlier + jnp.where(seq >= back, count, 0)
    turn_start = jnp.maximum(seq - 2, 0) * BLOCK + earlier

    def along_rows(row):
        wide = jnp.broadcast_to(row.astype(jnp.float32), (BLOCK, BLOCK))
        return jnp.transpose(wide).astype(jnp.int32)

    starts[0] = along_rows(doc_start)
    starts[1] = along_rows(turn_start)
    key_lanes = lax.broadcasted_iota(jnp.int32, (BLOCK, BLOCK), 1)
    query_places = seq * BLOCK + lax.broadcasted_iota(jnp.int32, (BLOCK, BLOCK), 0)

    for group in range(GROUPS):
        rows = slice(group * BLOCK, (group + 1) * BLOCK)
        q_rows[rows, :] = q_ref[:, group * HEAD_DIM : (group + 1) * HEAD_DIM]
    best[...] = jnp.full_like(best, MASKED)
    summed[...] = jnp.zeros_like(summed)

    def attend(stream, step):
        on, row = active(stream, step)

        @pl.when(on)
        def _():
            relay_copy(stream, row, y_far, 0, right).wait_recv()
            relay_copy(stream, row, y_far, 1, left).wait_recv()
            first = row * NY + (xh * (NZ * NY) if stream == UP else 0)
            for column in range(NY):
                block = first + column
                kept = (mask_ref[0, block] == 1) | (block == seq)
                low = jnp.maximum(starts[0], jnp.where(kept, 0, starts[1]))
                places = block * BLOCK + key_lanes
                allowed = (places >= low) & (places <= query_places)
                bias[:, pl.ds(column * BLOCK, BLOCK)] = jnp.where(allowed, 0.0, MASKED)
            keys = jnp.concatenate([kv[stream, row, c, 0] for c in range(NY)], axis=0)
            values = jnp.concatenate([kv[stream, row, c, 1] for c in range(NY)], axis=0)
            values = jnp.concatenate([values, jnp.ones_like(values)], axis=1)
            for start in range(0, GROUPS, HEADS):
                heads = min(HEADS, GROUPS - start)
                rows = pl.ds(start * BLOCK, heads * BLOCK)
                scores = lax.dot_general(
                    q_rows[rows, :],
                    keys,
                    (((1,), (1,)), ((), ())),
                    preferred_element_type=jnp.float32,
                )
                scores = scores.reshape(heads, BLOCK, NY * BLOCK) + bias[...][None]
                scores = scores.reshape(heads * BLOCK, NY * BLOCK)
                previous = best[rows, :]
                newest = jnp.maximum(previous, jnp.max(scores, axis=1, keepdims=True))
                factor = jnp.exp2((previous - newest) * FACTOR)
                weights = jnp.exp2((scores - newest) * FACTOR)
                best[rows, :] = newest
                summed[rows, :] = summed[rows, :] * factor + jnp.dot(
                    weights.astype(jnp.bfloat16), values, preferred_element_type=jnp.float32
                )

    def advance(step, carry):
        @pl.when(step < NZ)
        def _():
            forward(UP, step)
            forward(DOWN, step)
            column_send(step, lambda copy: copy.wait_send())

        column_send(step + WINDOW, lambda copy: copy.start())
        relay(UP, step - RELAY_LAG)
        relay(DOWN, step - RELAY_LAG)
        attend(UP, step - ATTEND_LAG)
        attend(DOWN, step - ATTEND_LAG)
        return carry

    lax.fori_loop(0, NZ + ATTEND_LAG, advance, 0)

    for group in range(GROUPS):
        rows = slice(group * BLOCK, (group + 1) * BLOCK)
        attended[:, group * HEAD_DIM : (group + 1) * HEAD_DIM] = (
            summed[rows, :HEAD_DIM] / summed[rows, HEAD_DIM:]
        ).astype(jnp.bfloat16)
    for part in range(NHEAD):
        weight_copy(part).wait()

    def project(part, start, width):
        return jnp.dot(
            attended[...],
            w[part, :, pl.ds(start, width)],
            preferred_element_type=jnp.float32,
        )

    def sibling_copy(index):
        start, width = CHUNKS[index % 2]
        place = index // 2
        return pltpu.make_async_remote_copy(
            src_ref=rs_out.at[place, :, pl.ds(start, width)],
            dst_ref=rs_in.at[place, :, pl.ds(start, width)],
            send_sem=rs_send.at[index],
            recv_sem=rs_recv.at[index],
            device_id=sibling,
            device_id_type=MESH,
        )

    def cross_copy(index):
        start, width = CHUNKS[index]
        return pltpu.make_async_remote_copy(
            src_ref=cross_out.at[:, pl.ds(start, width)],
            dst_ref=cross_in.at[:, pl.ds(start, width)],
            send_sem=cross_send.at[index],
            recv_sem=cross_recv.at[index],
            device_id=across,
            device_id_type=MESH,
        )

    far = 1 - chip
    for index, (start, width) in enumerate(CHUNKS):
        rs_out[0, :, pl.ds(start, width)] = project(far * 2 + 1 - core, start, width).astype(
            jnp.bfloat16
        )
        sibling_copy(index).start()
    for index, (start, width) in enumerate(CHUNKS):
        mine = project(far * 2 + core, start, width)
        sibling_copy(index).wait_recv()
        cross_out[:, pl.ds(start, width)] = (
            mine + rs_in[0, :, pl.ds(start, width)].astype(jnp.float32)
        ).astype(jnp.bfloat16)
        cross_copy(index).start()
    for index, (start, width) in enumerate(CHUNKS):
        rs_out[1, :, pl.ds(start, width)] = project(chip * 2 + 1 - core, start, width).astype(
            jnp.bfloat16
        )
        sibling_copy(2 + index).start()
    for index, (start, width) in enumerate(CHUNKS):
        mine = project(head, start, width)
        sibling_copy(2 + index).wait_recv()
        mine = mine + rs_in[1, :, pl.ds(start, width)].astype(jnp.float32)
        cross_copy(index).wait_recv()
        out_ref[:, pl.ds(start, width)] = (
            mine + cross_in[:, pl.ds(start, width)].astype(jnp.float32)
        ).astype(jnp.bfloat16)

    for index in range(4):
        sibling_copy(index).wait_send()
    for index in range(2):
        cross_copy(index).wait_send()

    def finish(step, carry):
        drain(UP, step)
        drain(DOWN, step)
        return carry

    lax.fori_loop(0, NZ, finish, 0)


def on_device(
    queries, key_codes, value_codes, kv_scales, out_weight, turn_ids, block_mask, doc_lengths
):
    dma = pltpu.SemaphoreType.DMA
    return pl.pallas_call(
        kernel,
        out_shape=jax.ShapeDtypeStruct(queries.shape, jnp.bfloat16),
        in_specs=[pl.BlockSpec(memory_space=pltpu.HBM)] * 8,
        out_specs=pl.BlockSpec(memory_space=pltpu.VMEM),
        scratch_shapes=[
            pltpu.VMEM(queries.shape, jnp.bfloat16),
            pltpu.VMEM(key_codes.shape, jnp.bfloat16),
            pltpu.VMEM(value_codes.shape, jnp.bfloat16),
            pltpu.SMEM((2,), jnp.float32),
            pltpu.VMEM((turn_ids.shape[0] // BLOCK, BLOCK), jnp.int32),
            pltpu.SMEM(block_mask.shape, jnp.int32),
            pltpu.SMEM(doc_lengths.shape, jnp.int32),
            pltpu.VMEM((2, NZ, NY, 2, BLOCK, HEAD_DIM), jnp.bfloat16),
            pltpu.VMEM((GROUPS * BLOCK, HEAD_DIM), jnp.bfloat16),
            pltpu.VMEM((NHEAD, WIDTH, WIDTH), jnp.bfloat16),
            pltpu.VMEM((BLOCK, NY * BLOCK), jnp.float32),
            pltpu.VMEM((2, BLOCK, BLOCK), jnp.int32),
            pltpu.VMEM((GROUPS * BLOCK, 1), jnp.float32),
            pltpu.VMEM((GROUPS * BLOCK, 2 * HEAD_DIM), jnp.float32),
            pltpu.VMEM((BLOCK, WIDTH), jnp.bfloat16),
            pltpu.VMEM((2, BLOCK, WIDTH), jnp.bfloat16),
            pltpu.VMEM((2, BLOCK, WIDTH), jnp.bfloat16),
            pltpu.VMEM((BLOCK, WIDTH), jnp.bfloat16),
            pltpu.VMEM((BLOCK, WIDTH), jnp.bfloat16),
            dma((NHEAD,)),
            dma((7,)),
            dma((2, NZ)),
            dma((2, NZ)),
            dma((2, NZ, 2)),
            dma((2, NZ, 2)),
            dma((2, NZ, 2)),
            dma((2, NZ, 2)),
            dma((4,)),
            dma((4,)),
            dma((2,)),
            dma((2,)),
        ],
        compiler_params=pltpu.CompilerParams(
            collective_id=0, has_side_effects=True, vmem_limit_bytes=40 * 1024 * 1024
        ),
    )(
        *(
            pltpu.with_memory_space_constraint(operand, pltpu.HBM)
            for operand in (
                queries,
                key_codes,
                value_codes,
                kv_scales.reshape(2),
                out_weight,
                turn_ids.reshape(-1, BLOCK),
                block_mask,
                doc_lengths,
            )
        )
    )


def solution(mesh):
    placed = (
        P("seq", "head"),
        P("seq", "head"),
        P("seq", "head"),
        P(None, "seq", "head"),
        P("head", None),
        P(),
        P("seq", None),
        P(),
    )
    return jax.shard_map(
        on_device, mesh=mesh, in_specs=placed, out_specs=P("seq", "head"), check_vma=False
    )
```

```python
import math

import jax
import jax.numpy as jnp
from jax import lax
from jax.experimental import pallas as pl
from jax.experimental.pallas import tpu as pltpu
from jax.sharding import PartitionSpec as P

HEAD_DIM = 128
BLOCK = 128
GROUPS = 7
WIDTH = GROUPS * HEAD_DIM
NX, NZ, NY = 2, 8, 4
PAIRS = NZ // 2
NHEAD = 4
MASKED = -1e30
FACTOR = math.log2(math.e) / math.sqrt(HEAD_DIM)
MESH = pl.DeviceIdType.MESH
UP, DOWN = 0, 1
WINDOW, SHARE_LAG, ATTEND_LAG = 2, 1, 2
HEADS = 2
PARTS = -(-GROUPS // HEADS)
CHUNKS = ((0, 512), (512, 384))


def kernel(
    q_hbm,
    kc_hbm,
    vc_hbm,
    scale_hbm,
    w_ref,
    turn_hbm,
    mask_hbm,
    doc_hbm,
    out_ref,
    q_ref,
    kc_ref,
    vc_ref,
    scale_ref,
    turn_ref,
    mask_ref,
    doc_ref,
    own,
    kv,
    q_rows,
    w,
    bias,
    starts,
    best,
    summed,
    result,
    attended,
    rs_out,
    rs_in,
    cross_out,
    cross_in,
    w_sem,
    in_sem,
    send_z,
    recv_z,
    send_y,
    recv_y,
    send_core,
    recv_core,
    swap_send,
    swap_recv,
    rs_send,
    rs_recv,
    cross_send,
    cross_recv,
):
    seq = lax.axis_index("seq")
    head = lax.axis_index("head")
    xh = seq // (NZ * NY)
    z = (seq // NY) % NZ
    y = seq % NY

    chip = head // 2
    core = head % 2
    pair = z // 2
    parity = z % 2
    home = core == parity
    row = pair * 2 + core
    query_seq = xh * (NZ * NY) + row * NY + y

    def at(to_xh, to_z, to_y, to_core):
        return (to_xh * (NZ * NY) + to_z * NY + to_y, chip * 2 + to_core)

    left = at(xh, z, (y + NY - 1) % NY, core)
    right = at(xh, z, (y + 1) % NY, core)
    opposite = at(xh, z, (y + 2) % NY, core)
    sibling = at(xh, z, y, 1 - core)
    partner = at(xh, z + 1 - 2 * parity, y, 1 - core)
    across = (seq, (1 - chip) * 2 + core)

    barrier = pltpu.get_barrier_semaphore()

    def greet(device):
        pl.semaphore_signal(barrier, inc=1, device_id=device, device_id_type=MESH)

    for device in (left, right, opposite, across):
        greet(device)
    for half in range(NX):
        for index in range(PAIRS):
            greet(at(half, 2 * index + 1 - core, y, parity))
            for to_core in range(2):

                @pl.when((half != xh) | (2 * index + core != z) | (to_core != core))
                def _():
                    greet(at(half, 2 * index + core, y, to_core))

    greeted = 4 + 3 * NX * PAIRS - jnp.where(home, 1, 0)

    def weight_copy(part):
        return pltpu.make_async_copy(
            w_ref.at[:, pl.ds(part * WIDTH, WIDTH)], w.at[part], w_sem.at[part]
        )

    staged = (
        (kc_hbm, kc_ref),
        (vc_hbm, vc_ref),
        (scale_hbm, scale_ref),
        (doc_hbm, doc_ref),
        (turn_hbm, turn_ref),
    )
    stage = [
        pltpu.make_async_copy(source, target, in_sem.at[index])
        for index, (source, target) in enumerate(staged)
    ]
    for copy in stage:
        copy.start()
    for copy in stage[:3]:
        copy.wait()

    own[0] = (kc_ref[...].astype(jnp.float32) * scale_ref[0]).astype(jnp.bfloat16)
    own[1] = (vc_ref[...].astype(jnp.float32) * scale_ref[1]).astype(jnp.bfloat16)

    @pl.when(home)
    def _():
        kv[UP, pair, y, core, parity] = own[core]

    pl.semaphore_wait(barrier, greeted)

    def column_copy(stream, step, half):
        to_xh, to_pair = (xh, pair + step) if stream == UP else (1 - xh, pair - step)
        return pltpu.make_async_remote_copy(
            src_ref=own.at[half],
            dst_ref=kv.at[stream, pair, y, half, parity],
            send_sem=send_z.at[stream, step, half],
            recv_sem=recv_z.at[stream, pair, parity],
            device_id=at(to_xh, (2 * to_pair + core + NZ) % NZ, y, half),
            device_id_type=MESH,
        )

    def arrival(stream, source, source_parity):
        return pltpu.make_async_remote_copy(
            src_ref=own.at[0],
            dst_ref=kv.at[stream, source, y, core, source_parity],
            send_sem=send_z.at[stream, 0, 0],
            recv_sem=recv_z.at[stream, source, source_parity],
            device_id=sibling,
            device_id_type=MESH,
        )

    def part_of(index):
        return pl.ds(index * HEADS * HEAD_DIM, min(HEADS, GROUPS - index * HEADS) * HEAD_DIM)

    swapped = [(mask_hbm, mask_ref), (q_hbm, q_ref)]
    swapped += [
        (result.at[:, part_of(index)], attended.at[:, part_of(index)]) for index in range(PARTS)
    ]

    def swap_copy(index):
        source, target = swapped[index]
        return pltpu.make_async_remote_copy(
            src_ref=source,
            dst_ref=target,
            send_sem=swap_send.at[index],
            recv_sem=swap_recv.at[index],
            device_id=partner,
            device_id_type=MESH,
        )

    def local_copy(index):
        source, target = swapped[index]
        return pltpu.make_async_copy(source, target, in_sem.at[len(staged) + index])

    def y_copy(stream, source, column, target, side):
        return pltpu.make_async_remote_copy(
            src_ref=kv.at[stream, source, column, core],
            dst_ref=kv.at[stream, source, column, core],
            send_sem=send_y.at[stream, source, side],
            recv_sem=recv_y.at[stream, source, side],
            device_id=target,
            device_id_type=MESH,
        )

    def core_copy(stream, source, column, side, half):
        return pltpu.make_async_remote_copy(
            src_ref=kv.at[stream, source, column, half],
            dst_ref=kv.at[stream, source, column, half],
            send_sem=send_core.at[stream, source, side],
            recv_sem=recv_core.at[stream, source, side],
            device_id=sibling,
            device_id_type=MESH,
        )

    y_left = (y + NY - 1) % NY
    y_right = (y + 1) % NY
    y_far = (y + 2) % NY

    sides = ((right, y_left), (left, y_right), (opposite, y_far))
    columns = (y_left, y_right, y_far, y)

    def active(stream, step):
        if stream == UP:
            return (step >= 0) & (step <= pair), pair - step
        return (xh == 1) & (step >= 0) & (step < PAIRS - pair), pair + step

    def column_send(step, act):
        for half in range(2):

            @pl.when((xh == 0) & (step <= pair))
            def _():
                act(column_copy(DOWN, step, half))

            @pl.when((pair + step < PAIRS) & ((step > 0) | (core != parity) | (core != half)))
            def _():
                act(column_copy(UP, step, half))

    def forward(stream, step):
        on, source = active(stream, step)

        @pl.when(on)
        def _():
            for source_parity in range(2):
                if stream == UP:

                    @pl.when((step > 0) | (core != parity) | (core != source_parity))
                    def _():
                        arrival(stream, source, source_parity).wait_recv()
                else:
                    arrival(stream, source, source_parity).wait_recv()
            for side, (target, _) in enumerate(sides):
                y_copy(stream, source, y, target, side).start()
            core_copy(stream, source, y, 3, core).start()

    for step in range(WINDOW):
        column_send(step, lambda copy: copy.start())

    def share(stream, step):
        on, source = active(stream, step)

        @pl.when(on)
        def _():
            for side, (target, column) in enumerate(sides):
                y_copy(stream, source, column, target, side).wait_recv()
                core_copy(stream, source, column, side, core).start()

    def drain(stream, step):
        on, source = active(stream, step)

        @pl.when(on)
        def _():
            for side, (target, _) in enumerate(sides):
                y_copy(stream, source, y, target, side).wait_send()
            for side, column in enumerate(columns):
                core_copy(stream, source, column, side, core).wait_send()

    forward(UP, 0)
    forward(DOWN, 0)

    @pl.when(home)
    def _():
        for index in range(2):
            local_copy(index).start()

    @pl.when(core != parity)
    def _():
        for index in range(2):
            swap_copy(index).start()

    if WINDOW < PAIRS:
        column_send(WINDOW, lambda copy: copy.start())
    for part in range(NHEAD):
        weight_copy(part).start()

    for copy in stage[3:]:
        copy.wait()

    lanes = lax.broadcasted_iota(jnp.int32, (1, BLOCK), 1)
    places = query_seq * BLOCK + lanes
    doc_start = jnp.zeros((1, BLOCK), jnp.int32)
    end = doc_ref[0]
    for index in range(doc_ref.shape[0]):
        doc_start = jnp.where(places >= end, end, doc_start)
        if index + 1 < doc_ref.shape[0]:
            end = end + doc_ref[index + 1]
    own_turns = turn_ref[pl.ds(query_seq, 1), :]
    earlier = jnp.zeros((1, BLOCK), jnp.int32)
    for back in range(3):
        block = jnp.maximum(query_seq - back, 0)
        turns = turn_ref[pl.ds(block, 1), :].astype(jnp.float32)
        column = jnp.transpose(jnp.broadcast_to(turns, (BLOCK, BLOCK))).astype(jnp.int32)
        count = jnp.sum(jnp.where(column < own_turns, 1, 0), axis=0, keepdims=True)
        earlier = earlier + jnp.where(query_seq >= back, count, 0)
    turn_start = jnp.maximum(query_seq - 2, 0) * BLOCK + earlier

    def along_rows(row):
        wide = jnp.broadcast_to(row.astype(jnp.float32), (BLOCK, BLOCK))
        return jnp.transpose(wide).astype(jnp.int32)

    starts[0] = along_rows(doc_start)
    starts[1] = along_rows(turn_start)
    key_lanes = lax.broadcasted_iota(jnp.int32, (BLOCK, BLOCK), 1)
    mask_lanes = lax.broadcasted_iota(jnp.int32, mask_ref.shape, 1)
    query_places = query_seq * BLOCK + lax.broadcasted_iota(jnp.int32, (BLOCK, BLOCK), 0)

    best[...] = jnp.full_like(best, MASKED)
    summed[...] = jnp.zeros_like(summed)

    def divide(index, target):
        for group in range(index * HEADS, min((index + 1) * HEADS, GROUPS)):
            rows = slice(group * BLOCK, (group + 1) * BLOCK)
            target[:, group * HEAD_DIM : (group + 1) * HEAD_DIM] = (
                summed[rows, :HEAD_DIM] / summed[rows, HEAD_DIM:]
            ).astype(jnp.bfloat16)

    def attend(stream, step):
        on, source = active(stream, step)
        @pl.when(on)
        def _():
            for side, column in enumerate(columns):
                core_copy(stream, source, column, side, 1 - core).wait_recv()
            for index in range(2 * NY):
                block = (source * 2 + index // NY) * NY + index % NY
                if stream == UP:
                    block = block + xh * (NZ * NY)
                kept = jnp.sum(
                    jnp.where(mask_lanes == block, mask_ref[...], 0), axis=1, keepdims=True
                )
                same = jnp.where(block == query_seq, 1, 0)
                low = jnp.maximum(starts[0], starts[1] * (1 - jnp.maximum(kept, same)))
                places = block * BLOCK + key_lanes
                allowed = (places >= low) & (places <= query_places)
                bias[:, pl.ds(index * BLOCK, BLOCK)] = jnp.where(allowed, 0.0, MASKED)
            blocks = [(index % NY, index // NY) for index in range(2 * NY)]
            keys = jnp.concatenate([kv[stream, source, c, 0, r] for c, r in blocks], axis=0)
            values = jnp.concatenate([kv[stream, source, c, 1, r] for c, r in blocks], axis=0)
            values = jnp.concatenate([values, jnp.ones_like(values)], axis=1)
            for start in range(0, GROUPS, HEADS):
                heads = min(HEADS, GROUPS - start)
                rows = pl.ds(start * BLOCK, heads * BLOCK)
                scores = lax.dot_general(
                    q_rows[rows, :],
                    keys,
                    (((1,), (1,)), ((), ())),
                    preferred_element_type=jnp.float32,
                )
                scores = scores.reshape(heads, BLOCK, 2 * NY * BLOCK) + bias[...][None]
                scores = scores.reshape(heads * BLOCK, 2 * NY * BLOCK)
                previous = best[rows, :]
                newest = jnp.maximum(previous, jnp.max(scores, axis=1, keepdims=True))
                factor = jnp.exp2((previous - newest) * FACTOR)
                weights = jnp.exp2((scores - newest) * FACTOR)
                best[rows, :] = newest
                summed[rows, :] = summed[rows, :] * factor + jnp.dot(
                    weights.astype(jnp.bfloat16), values, preferred_element_type=jnp.float32
                )

    def take_queries():
        @pl.when(home)
        def _():
            for index in range(2):
                local_copy(index).wait()

        @pl.when(core != parity)
        def _():
            for index in range(2):
                swap_copy(index).wait_recv()

        for group in range(GROUPS):
            rows = slice(group * BLOCK, (group + 1) * BLOCK)
            q_rows[rows, :] = q_ref[:, group * HEAD_DIM : (group + 1) * HEAD_DIM]

    def advance(step, carry):
        @pl.when(step > 0)
        def _():
            forward(UP, step)
            forward(DOWN, step)
            if WINDOW < PAIRS:
                column_send(step + WINDOW, lambda copy: copy.start())

        @pl.when(step == ATTEND_LAG)
        def _():
            take_queries()

        attend(UP, step - ATTEND_LAG)
        attend(DOWN, step - ATTEND_LAG)
        share(UP, step - SHARE_LAG)
        share(DOWN, step - SHARE_LAG)
        return carry

    lax.fori_loop(0, PAIRS + ATTEND_LAG, advance, 0)

    @pl.when(home)
    def _():
        for index in range(PARTS):
            divide(index, attended)

    @pl.when(core != parity)
    def _():
        for index in range(PARTS):
            divide(index, result)
            swap_copy(2 + index).start()

    @pl.when(core != parity)
    def _():
        for index in range(PARTS):
            swap_copy(2 + index).wait_recv()

    for part in range(NHEAD):
        weight_copy(part).wait()

    def project(part, start, width):
        return jnp.dot(
            attended[...],
            w[part, :, pl.ds(start, width)],
            preferred_element_type=jnp.float32,
        )

    def sibling_copy(index):
        start, width = CHUNKS[index % len(CHUNKS)]
        place = index // len(CHUNKS)
        return pltpu.make_async_remote_copy(
            src_ref=rs_out.at[place, :, pl.ds(start, width)],
            dst_ref=rs_in.at[place, :, pl.ds(start, width)],
            send_sem=rs_send.at[index],
            recv_sem=rs_recv.at[index],
            device_id=sibling,
            device_id_type=MESH,
        )

    def cross_copy(index):
        start, width = CHUNKS[index]
        return pltpu.make_async_remote_copy(
            src_ref=cross_out.at[:, pl.ds(start, width)],
            dst_ref=cross_in.at[:, pl.ds(start, width)],
            send_sem=cross_send.at[index],
            recv_sem=cross_recv.at[index],
            device_id=across,
            device_id_type=MESH,
        )

    far = 1 - chip
    for index, (start, width) in enumerate(CHUNKS):
        rs_out[0, :, pl.ds(start, width)] = project(far * 2 + 1 - core, start, width).astype(
            jnp.bfloat16
        )
        sibling_copy(index).start()
    for index, (start, width) in enumerate(CHUNKS):
        mine = project(far * 2 + core, start, width)
        sibling_copy(index).wait_recv()
        cross_out[:, pl.ds(start, width)] = (
            mine + rs_in[0, :, pl.ds(start, width)].astype(jnp.float32)
        ).astype(jnp.bfloat16)
        cross_copy(index).start()
    for index, (start, width) in enumerate(CHUNKS):
        rs_out[1, :, pl.ds(start, width)] = project(chip * 2 + 1 - core, start, width).astype(
            jnp.bfloat16
        )
        sibling_copy(len(CHUNKS) + index).start()
    for index, (start, width) in enumerate(CHUNKS):
        mine = project(head, start, width)
        sibling_copy(len(CHUNKS) + index).wait_recv()
        mine = mine + rs_in[1, :, pl.ds(start, width)].astype(jnp.float32)
        cross_copy(index).wait_recv()
        out_ref[:, pl.ds(start, width)] = (
            mine + cross_in[:, pl.ds(start, width)].astype(jnp.float32)
        ).astype(jnp.bfloat16)

    for index in range(2 * len(CHUNKS)):
        sibling_copy(index).wait_send()
    for index in range(len(CHUNKS)):
        cross_copy(index).wait_send()

    def finish(step, carry):
        drain(UP, step)
        drain(DOWN, step)
        return carry

    lax.fori_loop(0, PAIRS, finish, 0)
    for step in range(PAIRS):
        column_send(step, lambda copy: copy.wait_send())

    @pl.when(core != parity)
    def _():
        for index in range(2 + PARTS):
            swap_copy(index).wait_send()


def on_device(
    queries, key_codes, value_codes, kv_scales, out_weight, turn_ids, block_mask, doc_lengths
):
    dma = pltpu.SemaphoreType.DMA
    return pl.pallas_call(
        kernel,
        out_shape=jax.ShapeDtypeStruct(queries.shape, jnp.bfloat16),
        in_specs=[pl.BlockSpec(memory_space=pltpu.HBM)] * 8,
        out_specs=pl.BlockSpec(memory_space=pltpu.VMEM),
        scratch_shapes=[
            pltpu.VMEM(queries.shape, jnp.bfloat16),
            pltpu.VMEM(key_codes.shape, jnp.bfloat16),
            pltpu.VMEM(value_codes.shape, jnp.bfloat16),
            pltpu.SMEM((2,), jnp.float32),
            pltpu.VMEM((turn_ids.shape[0] // BLOCK, BLOCK), jnp.int32),
            pltpu.VMEM(block_mask.shape, jnp.int32),
            pltpu.SMEM(doc_lengths.shape, jnp.int32),
            pltpu.VMEM((2, BLOCK, HEAD_DIM), jnp.bfloat16),
            pltpu.VMEM((2, PAIRS, NY, 2, 2, BLOCK, HEAD_DIM), jnp.bfloat16),
            pltpu.VMEM((GROUPS * BLOCK, HEAD_DIM), jnp.bfloat16),
            pltpu.VMEM((NHEAD, WIDTH, WIDTH), jnp.bfloat16),
            pltpu.VMEM((BLOCK, 2 * NY * BLOCK), jnp.float32),
            pltpu.VMEM((2, BLOCK, BLOCK), jnp.int32),
            pltpu.VMEM((GROUPS * BLOCK, 1), jnp.float32),
            pltpu.VMEM((GROUPS * BLOCK, 2 * HEAD_DIM), jnp.float32),
            pltpu.VMEM((BLOCK, WIDTH), jnp.bfloat16),
            pltpu.VMEM((BLOCK, WIDTH), jnp.bfloat16),
            pltpu.VMEM((2, BLOCK, WIDTH), jnp.bfloat16),
            pltpu.VMEM((2, BLOCK, WIDTH), jnp.bfloat16),
            pltpu.VMEM((BLOCK, WIDTH), jnp.bfloat16),
            pltpu.VMEM((BLOCK, WIDTH), jnp.bfloat16),
            dma((NHEAD,)),
            dma((7,)),
            dma((2, PAIRS, 2)),
            dma((2, PAIRS, 2)),
            dma((2, PAIRS, 3)),
            dma((2, PAIRS, 3)),
            dma((2, PAIRS, 4)),
            dma((2, PAIRS, 4)),
            dma((2 + PARTS,)),
            dma((2 + PARTS,)),
            dma((2 * len(CHUNKS),)),
            dma((2 * len(CHUNKS),)),
            dma((len(CHUNKS),)),
            dma((len(CHUNKS),)),
        ],
        compiler_params=pltpu.CompilerParams(
            collective_id=0, has_side_effects=True, vmem_limit_bytes=40 * 1024 * 1024
        ),
    )(
        *(
            pltpu.with_memory_space_constraint(operand, pltpu.HBM)
            for operand in (
                queries,
                key_codes,
                value_codes,
                kv_scales.reshape(2),
                out_weight,
                turn_ids.reshape(-1, BLOCK),
                block_mask,
                doc_lengths,
            )
        )
    )


def solution(mesh):
    placed = (
        P("seq", "head"),
        P("seq", "head"),
        P("seq", "head"),
        P(None, "seq", "head"),
        P("head", None),
        P(),
        P("seq", None),
        P(),
    )
    return jax.shard_map(
        on_device, mesh=mesh, in_specs=placed, out_specs=P("seq", "head"), check_vma=False
    )
```

```python
import math

import jax
import jax.numpy as jnp
from jax import lax
from jax.experimental import pallas as pl
from jax.experimental.pallas import tpu as pltpu
from jax.sharding import PartitionSpec as P

HEAD_DIM = 128
BLOCK = 128
GROUPS = 7
WIDTH = GROUPS * HEAD_DIM
NX, NZ, NY = 2, 8, 4
PAIRS = NZ // 2
NHEAD = 4
MASKED = -1e30
FACTOR = math.log2(math.e) / math.sqrt(HEAD_DIM)
MESH = pl.DeviceIdType.MESH
UP, DOWN = 0, 1
WINDOW, SHARE_LAG, ATTEND_LAG = 2, 1, 2
HEADS = 2
PARTS = -(-GROUPS // HEADS)
CHUNKS = ((0, 512), (512, 384))


def kernel(
    q_hbm,
    kc_hbm,
    vc_hbm,
    scale_hbm,
    w_ref,
    turn_hbm,
    mask_hbm,
    doc_hbm,
    out_ref,
    q_ref,
    kc_ref,
    vc_ref,
    scale_ref,
    turn_ref,
    mask_ref,
    doc_ref,
    own,
    kv,
    q_rows,
    w,
    bias,
    starts,
    best,
    summed,
    result,
    attended,
    rs_out,
    rs_in,
    cross_out,
    cross_in,
    w_sem,
    in_sem,
    send_z,
    recv_z,
    send_y,
    recv_y,
    send_core,
    recv_core,
    swap_send,
    swap_recv,
    rs_send,
    rs_recv,
    cross_send,
    cross_recv,
):
    seq = lax.axis_index("seq")
    head = lax.axis_index("head")
    xh = seq // (NZ * NY)
    z = (seq // NY) % NZ
    y = seq % NY

    chip = head // 2
    core = head % 2
    pair = z // 2
    parity = z % 2
    home = core == parity
    row = pair * 2 + core
    query_seq = xh * (NZ * NY) + row * NY + y

    def at(to_xh, to_z, to_y, to_core):
        return (to_xh * (NZ * NY) + to_z * NY + to_y, chip * 2 + to_core)

    left = at(xh, z, (y + NY - 1) % NY, core)
    right = at(xh, z, (y + 1) % NY, core)
    opposite = at(xh, z, (y + 2) % NY, core)
    sibling = at(xh, z, y, 1 - core)
    partner = at(xh, z + 1 - 2 * parity, y, 1 - core)
    across = (seq, (1 - chip) * 2 + core)

    barrier = pltpu.get_barrier_semaphore()

    def greet(device):
        pl.semaphore_signal(barrier, inc=1, device_id=device, device_id_type=MESH)

    for device in (left, right, opposite, across):
        greet(device)
    for half in range(NX):
        for index in range(PAIRS):
            greet(at(half, 2 * index + 1 - core, y, parity))
            for to_core in range(2):

                @pl.when((half != xh) | (2 * index + core != z) | (to_core != core))
                def _():
                    greet(at(half, 2 * index + core, y, to_core))

    greeted = 4 + 3 * NX * PAIRS - jnp.where(home, 1, 0)

    def weight_copy(part):
        return pltpu.make_async_copy(
            w_ref.at[:, pl.ds(part * WIDTH, WIDTH)], w.at[part], w_sem.at[part]
        )

    staged = (
        (kc_hbm, kc_ref),
        (vc_hbm, vc_ref),
        (scale_hbm, scale_ref),
        (doc_hbm, doc_ref),
        (turn_hbm, turn_ref),
    )
    stage = [
        pltpu.make_async_copy(source, target, in_sem.at[index])
        for index, (source, target) in enumerate(staged)
    ]
    for copy in stage:
        copy.start()
    for copy in stage[:3]:
        copy.wait()

    own[0] = (kc_ref[...].astype(jnp.float32) * scale_ref[0]).astype(jnp.bfloat16)
    own[1] = (vc_ref[...].astype(jnp.float32) * scale_ref[1]).astype(jnp.bfloat16)

    @pl.when(home)
    def _():
        kv[UP, pair, y, core, parity] = own[core]

    pl.semaphore_wait(barrier, greeted)

    def column_copy(stream, step, half):
        to_xh, to_pair = (xh, pair + step) if stream == UP else (1 - xh, pair - step)
        return pltpu.make_async_remote_copy(
            src_ref=own.at[half],
            dst_ref=kv.at[stream, pair, y, half, parity],
            send_sem=send_z.at[stream, step, half],
            recv_sem=recv_z.at[stream, pair, parity],
            device_id=at(to_xh, (2 * to_pair + core + NZ) % NZ, y, half),
            device_id_type=MESH,
        )

    def arrival(stream, source, source_parity):
        return pltpu.make_async_remote_copy(
            src_ref=own.at[0],
            dst_ref=kv.at[stream, source, y, core, source_parity],
            send_sem=send_z.at[stream, 0, 0],
            recv_sem=recv_z.at[stream, source, source_parity],
            device_id=sibling,
            device_id_type=MESH,
        )

    def part_of(index):
        return pl.ds(index * HEADS * HEAD_DIM, min(HEADS, GROUPS - index * HEADS) * HEAD_DIM)

    swapped = [(mask_hbm, mask_ref), (q_hbm, q_ref)]
    swapped += [
        (result.at[:, part_of(index)], attended.at[:, part_of(index)]) for index in range(PARTS)
    ]

    def swap_copy(index):
        source, target = swapped[index]
        return pltpu.make_async_remote_copy(
            src_ref=source,
            dst_ref=target,
            send_sem=swap_send.at[index],
            recv_sem=swap_recv.at[index],
            device_id=partner,
            device_id_type=MESH,
        )

    def local_copy(index):
        source, target = swapped[index]
        return pltpu.make_async_copy(source, target, in_sem.at[len(staged) + index])

    def y_copy(stream, source, column, target, side):
        return pltpu.make_async_remote_copy(
            src_ref=kv.at[stream, source, column, core],
            dst_ref=kv.at[stream, source, column, core],
            send_sem=send_y.at[stream, source, side],
            recv_sem=recv_y.at[stream, source, side],
            device_id=target,
            device_id_type=MESH,
        )

    def core_copy(stream, source, column, side, half):
        return pltpu.make_async_remote_copy(
            src_ref=kv.at[stream, source, column, half],
            dst_ref=kv.at[stream, source, column, half],
            send_sem=send_core.at[stream, source, side],
            recv_sem=recv_core.at[stream, source, side],
            device_id=sibling,
            device_id_type=MESH,
        )

    y_left = (y + NY - 1) % NY
    y_right = (y + 1) % NY
    y_far = (y + 2) % NY

    sides = ((right, y_left), (left, y_right), (opposite, y_far))
    columns = (y_left, y_right, y_far, y)

    def active(stream, step):
        if stream == UP:
            return (step >= 0) & (step <= pair), pair - step
        return (xh == 1) & (step >= 0) & (step < PAIRS - pair), pair + step

    def column_send(step, act):
        for half in range(2):

            @pl.when((xh == 0) & (step <= pair))
            def _():
                act(column_copy(DOWN, step, half))

            @pl.when((pair + step < PAIRS) & ((step > 0) | (core != parity) | (core != half)))
            def _():
                act(column_copy(UP, step, half))

    def forward(stream, step):
        on, source = active(stream, step)

        @pl.when(on)
        def _():
            for source_parity in range(2):
                if stream == UP:

                    @pl.when((step > 0) | (core != parity) | (core != source_parity))
                    def _():
                        arrival(stream, source, source_parity).wait_recv()
                else:
                    arrival(stream, source, source_parity).wait_recv()
            for side in (2, 0, 1):
                y_copy(stream, source, y, sides[side][0], side).start()
            core_copy(stream, source, y, 3, core).start()

    for step in range(WINDOW):
        column_send(step, lambda copy: copy.start())

    def share(stream, step):
        on, source = active(stream, step)

        @pl.when(on)
        def _():
            for side, (target, column) in enumerate(sides):
                y_copy(stream, source, column, target, side).wait_recv()
                core_copy(stream, source, column, side, core).start()

    def drain(stream, step):
        on, source = active(stream, step)

        @pl.when(on)
        def _():
            for side, (target, _) in enumerate(sides):
                y_copy(stream, source, y, target, side).wait_send()
            for side, column in enumerate(columns):
                core_copy(stream, source, column, side, core).wait_send()

    forward(UP, 0)
    forward(DOWN, 0)

    @pl.when(home)
    def _():
        for index in range(2):
            local_copy(index).start()

    @pl.when(core != parity)
    def _():
        for index in range(2):
            swap_copy(index).start()

    if WINDOW < PAIRS:
        column_send(WINDOW, lambda copy: copy.start())
    for part in range(NHEAD):
        weight_copy(part).start()

    for copy in stage[3:]:
        copy.wait()

    lanes = lax.broadcasted_iota(jnp.int32, (1, BLOCK), 1)
    places = query_seq * BLOCK + lanes
    doc_start = jnp.zeros((1, BLOCK), jnp.int32)
    end = doc_ref[0]
    for index in range(doc_ref.shape[0]):
        doc_start = jnp.where(places >= end, end, doc_start)
        if index + 1 < doc_ref.shape[0]:
            end = end + doc_ref[index + 1]
    own_turns = turn_ref[pl.ds(query_seq, 1), :]
    earlier = jnp.zeros((1, BLOCK), jnp.int32)
    for back in range(3):
        block = jnp.maximum(query_seq - back, 0)
        turns = turn_ref[pl.ds(block, 1), :].astype(jnp.float32)
        column = jnp.transpose(jnp.broadcast_to(turns, (BLOCK, BLOCK))).astype(jnp.int32)
        count = jnp.sum(jnp.where(column < own_turns, 1, 0), axis=0, keepdims=True)
        earlier = earlier + jnp.where(query_seq >= back, count, 0)
    turn_start = jnp.maximum(query_seq - 2, 0) * BLOCK + earlier

    def along_rows(row):
        wide = jnp.broadcast_to(row.astype(jnp.float32), (BLOCK, BLOCK))
        return jnp.transpose(wide).astype(jnp.int32)

    starts[0] = along_rows(doc_start)
    starts[1] = along_rows(turn_start)
    key_lanes = lax.broadcasted_iota(jnp.int32, (BLOCK, BLOCK), 1)
    mask_lanes = lax.broadcasted_iota(jnp.int32, mask_ref.shape, 1)
    query_places = query_seq * BLOCK + lax.broadcasted_iota(jnp.int32, (BLOCK, BLOCK), 0)

    best[...] = jnp.full_like(best, MASKED)
    summed[...] = jnp.zeros_like(summed)

    def divide(index, target):
        for group in range(index * HEADS, min((index + 1) * HEADS, GROUPS)):
            rows = slice(group * BLOCK, (group + 1) * BLOCK)
            target[:, group * HEAD_DIM : (group + 1) * HEAD_DIM] = (
                summed[rows, :HEAD_DIM] / summed[rows, HEAD_DIM:]
            ).astype(jnp.bfloat16)

    def attend_pair(stream, source, leaving):
        for side, column in enumerate(columns):
            core_copy(stream, source, column, side, 1 - core).wait_recv()
        for index in range(2 * NY):
            block = (source * 2 + index // NY) * NY + index % NY
            if stream == UP:
                block = block + xh * (NZ * NY)
            kept = jnp.sum(
                jnp.where(mask_lanes == block, mask_ref[...], 0), axis=1, keepdims=True
            )
            same = jnp.where(block == query_seq, 1, 0)
            low = jnp.maximum(starts[0], starts[1] * (1 - jnp.maximum(kept, same)))
            places = block * BLOCK + key_lanes
            allowed = (places >= low) & (places <= query_places)
            bias[:, pl.ds(index * BLOCK, BLOCK)] = jnp.where(allowed, 0.0, MASKED)
        blocks = [(index % NY, index // NY) for index in range(2 * NY)]
        keys = jnp.concatenate([kv[stream, source, c, 0, r] for c, r in blocks], axis=0)
        values = jnp.concatenate([kv[stream, source, c, 1, r] for c, r in blocks], axis=0)
        values = jnp.concatenate([values, jnp.ones_like(values)], axis=1)
        for start in range(0, GROUPS, HEADS):
            heads = min(HEADS, GROUPS - start)
            rows = pl.ds(start * BLOCK, heads * BLOCK)
            scores = lax.dot_general(
                q_rows[rows, :],
                keys,
                (((1,), (1,)), ((), ())),
                preferred_element_type=jnp.float32,
            )
            scores = scores.reshape(heads, BLOCK, 2 * NY * BLOCK) + bias[...][None]
            scores = scores.reshape(heads * BLOCK, 2 * NY * BLOCK)
            previous = best[rows, :]
            newest = jnp.maximum(previous, jnp.max(scores, axis=1, keepdims=True))
            factor = jnp.exp2((previous - newest) * FACTOR)
            weights = jnp.exp2((scores - newest) * FACTOR)
            best[rows, :] = newest
            summed[rows, :] = summed[rows, :] * factor + jnp.dot(
                weights.astype(jnp.bfloat16), values, preferred_element_type=jnp.float32
            )
            if leaving:
                divide(start // HEADS, result)
                swap_copy(2 + start // HEADS).start()

    def attend(stream, step):
        on, source = active(stream, step)
        down_last = (xh == 1) & (PAIRS - 1 - pair >= pair)
        if stream == UP:
            last = (step == pair) & jnp.logical_not(down_last)
        else:
            last = (step == PAIRS - 1 - pair) & down_last
        leaving = last & (core != parity)

        @pl.when(on & jnp.logical_not(leaving))
        def _():
            attend_pair(stream, source, False)

        @pl.when(on & leaving)
        def _():
            attend_pair(stream, source, True)

    def take_queries():
        @pl.when(home)
        def _():
            for index in range(2):
                local_copy(index).wait()

        @pl.when(core != parity)
        def _():
            for index in range(2):
                swap_copy(index).wait_recv()

        for group in range(GROUPS):
            rows = slice(group * BLOCK, (group + 1) * BLOCK)
            q_rows[rows, :] = q_ref[:, group * HEAD_DIM : (group + 1) * HEAD_DIM]

    def advance(step, carry):
        @pl.when(step > 0)
        def _():
            forward(UP, step)
            forward(DOWN, step)
            if WINDOW < PAIRS:
                column_send(step + WINDOW, lambda copy: copy.start())

        @pl.when(step == ATTEND_LAG)
        def _():
            take_queries()

        attend(UP, step - ATTEND_LAG)
        attend(DOWN, step - ATTEND_LAG)
        share(UP, step - SHARE_LAG)
        share(DOWN, step - SHARE_LAG)
        return carry

    lax.fori_loop(0, PAIRS + ATTEND_LAG, advance, 0)

    @pl.when(home)
    def _():
        for index in range(PARTS):
            divide(index, attended)

    @pl.when(core != parity)
    def _():
        for index in range(PARTS):
            swap_copy(2 + index).wait_recv()

    for part in range(NHEAD):
        weight_copy(part).wait()

    def project(part, start, width):
        return jnp.dot(
            attended[...],
            w[part, :, pl.ds(start, width)],
            preferred_element_type=jnp.float32,
        )

    def sibling_copy(index):
        start, width = CHUNKS[index % len(CHUNKS)]
        place = index // len(CHUNKS)
        return pltpu.make_async_remote_copy(
            src_ref=rs_out.at[place, :, pl.ds(start, width)],
            dst_ref=rs_in.at[place, :, pl.ds(start, width)],
            send_sem=rs_send.at[index],
            recv_sem=rs_recv.at[index],
            device_id=sibling,
            device_id_type=MESH,
        )

    def cross_copy(index):
        start, width = CHUNKS[index]
        return pltpu.make_async_remote_copy(
            src_ref=cross_out.at[:, pl.ds(start, width)],
            dst_ref=cross_in.at[:, pl.ds(start, width)],
            send_sem=cross_send.at[index],
            recv_sem=cross_recv.at[index],
            device_id=across,
            device_id_type=MESH,
        )

    far = 1 - chip
    for index, (start, width) in enumerate(CHUNKS):
        rs_out[0, :, pl.ds(start, width)] = project(far * 2 + 1 - core, start, width).astype(
            jnp.bfloat16
        )
        sibling_copy(index).start()
    for index, (start, width) in enumerate(CHUNKS):
        mine = project(far * 2 + core, start, width)
        sibling_copy(index).wait_recv()
        cross_out[:, pl.ds(start, width)] = (
            mine + rs_in[0, :, pl.ds(start, width)].astype(jnp.float32)
        ).astype(jnp.bfloat16)
        cross_copy(index).start()
    for index, (start, width) in enumerate(CHUNKS):
        rs_out[1, :, pl.ds(start, width)] = project(chip * 2 + 1 - core, start, width).astype(
            jnp.bfloat16
        )
        sibling_copy(len(CHUNKS) + index).start()
    for index, (start, width) in enumerate(CHUNKS):
        mine = project(head, start, width)
        sibling_copy(len(CHUNKS) + index).wait_recv()
        mine = mine + rs_in[1, :, pl.ds(start, width)].astype(jnp.float32)
        cross_copy(index).wait_recv()
        out_ref[:, pl.ds(start, width)] = (
            mine + cross_in[:, pl.ds(start, width)].astype(jnp.float32)
        ).astype(jnp.bfloat16)

    for index in range(2 * len(CHUNKS)):
        sibling_copy(index).wait_send()
    for index in range(len(CHUNKS)):
        cross_copy(index).wait_send()

    def finish(step, carry):
        drain(UP, step)
        drain(DOWN, step)
        return carry

    lax.fori_loop(0, PAIRS, finish, 0)
    for step in range(PAIRS):
        column_send(step, lambda copy: copy.wait_send())

    @pl.when(core != parity)
    def _():
        for index in range(2 + PARTS):
            swap_copy(index).wait_send()


def on_device(
    queries, key_codes, value_codes, kv_scales, out_weight, turn_ids, block_mask, doc_lengths
):
    dma = pltpu.SemaphoreType.DMA
    return pl.pallas_call(
        kernel,
        out_shape=jax.ShapeDtypeStruct(queries.shape, jnp.bfloat16),
        in_specs=[pl.BlockSpec(memory_space=pltpu.HBM)] * 8,
        out_specs=pl.BlockSpec(memory_space=pltpu.VMEM),
        scratch_shapes=[
            pltpu.VMEM(queries.shape, jnp.bfloat16),
            pltpu.VMEM(key_codes.shape, jnp.bfloat16),
            pltpu.VMEM(value_codes.shape, jnp.bfloat16),
            pltpu.SMEM((2,), jnp.float32),
            pltpu.VMEM((turn_ids.shape[0] // BLOCK, BLOCK), jnp.int32),
            pltpu.VMEM(block_mask.shape, jnp.int32),
            pltpu.SMEM(doc_lengths.shape, jnp.int32),
            pltpu.VMEM((2, BLOCK, HEAD_DIM), jnp.bfloat16),
            pltpu.VMEM((2, PAIRS, NY, 2, 2, BLOCK, HEAD_DIM), jnp.bfloat16),
            pltpu.VMEM((GROUPS * BLOCK, HEAD_DIM), jnp.bfloat16),
            pltpu.VMEM((NHEAD, WIDTH, WIDTH), jnp.bfloat16),
            pltpu.VMEM((BLOCK, 2 * NY * BLOCK), jnp.float32),
            pltpu.VMEM((2, BLOCK, BLOCK), jnp.int32),
            pltpu.VMEM((GROUPS * BLOCK, 1), jnp.float32),
            pltpu.VMEM((GROUPS * BLOCK, 2 * HEAD_DIM), jnp.float32),
            pltpu.VMEM((BLOCK, WIDTH), jnp.bfloat16),
            pltpu.VMEM((BLOCK, WIDTH), jnp.bfloat16),
            pltpu.VMEM((2, BLOCK, WIDTH), jnp.bfloat16),
            pltpu.VMEM((2, BLOCK, WIDTH), jnp.bfloat16),
            pltpu.VMEM((BLOCK, WIDTH), jnp.bfloat16),
            pltpu.VMEM((BLOCK, WIDTH), jnp.bfloat16),
            dma((NHEAD,)),
            dma((7,)),
            dma((2, PAIRS, 2)),
            dma((2, PAIRS, 2)),
            dma((2, PAIRS, 3)),
            dma((2, PAIRS, 3)),
            dma((2, PAIRS, 4)),
            dma((2, PAIRS, 4)),
            dma((2 + PARTS,)),
            dma((2 + PARTS,)),
            dma((2 * len(CHUNKS),)),
            dma((2 * len(CHUNKS),)),
            dma((len(CHUNKS),)),
            dma((len(CHUNKS),)),
        ],
        compiler_params=pltpu.CompilerParams(
            collective_id=0, has_side_effects=True, vmem_limit_bytes=40 * 1024 * 1024
        ),
    )(
        *(
            pltpu.with_memory_space_constraint(operand, pltpu.HBM)
            for operand in (
                queries,
                key_codes,
                value_codes,
                kv_scales.reshape(2),
                out_weight,
                turn_ids.reshape(-1, BLOCK),
                block_mask,
                doc_lengths,
            )
        )
    )


def solution(mesh):
    placed = (
        P("seq", "head"),
        P("seq", "head"),
        P("seq", "head"),
        P(None, "seq", "head"),
        P("head", None),
        P(),
        P("seq", None),
        P(),
    )
    return jax.shard_map(
        on_device, mesh=mesh, in_specs=placed, out_specs=P("seq", "head"), check_vma=False
    )
```

```python
import math

import jax
import jax.numpy as jnp
from jax import lax
from jax.experimental import pallas as pl
from jax.experimental.pallas import tpu as pltpu
from jax.sharding import PartitionSpec as P

HEAD_DIM = 128
BLOCK = 128
GROUPS = 7
WIDTH = GROUPS * HEAD_DIM
NX, NZ, NY = 2, 8, 4
PAIRS = NZ // 2
NHEAD = 4
MASKED = -1e30
FACTOR = math.log2(math.e) / math.sqrt(HEAD_DIM)
MESH = pl.DeviceIdType.MESH
UP, DOWN = 0, 1
WINDOW, SHARE_LAG, ATTEND_LAG = 2, 1, 2
HEADS = 2
PARTS = -(-GROUPS // HEADS)
CHUNKS = ((0, 512), (512, 384))


def kernel(
    q_hbm,
    kc_hbm,
    vc_hbm,
    scale_hbm,
    w_ref,
    turn_hbm,
    mask_hbm,
    doc_hbm,
    out_ref,
    q_ref,
    kc_ref,
    vc_ref,
    scale_ref,
    turn_ref,
    mask_ref,
    doc_ref,
    own,
    kv,
    q_rows,
    w,
    bias,
    starts,
    best,
    summed,
    result,
    attended,
    rs_out,
    rs_in,
    cross_out,
    cross_in,
    w_sem,
    in_sem,
    send_z,
    recv_z,
    send_y,
    recv_y,
    send_core,
    recv_core,
    swap_send,
    swap_recv,
    rs_send,
    rs_recv,
    cross_send,
    cross_recv,
):
    seq = lax.axis_index("seq")
    head = lax.axis_index("head")
    xh = seq // (NZ * NY)
    z = (seq // NY) % NZ
    y = seq % NY

    chip = head // 2
    core = head % 2
    pair = z // 2
    parity = z % 2
    home = core == parity
    row = pair * 2 + core
    query_seq = xh * (NZ * NY) + row * NY + y

    def at(to_xh, to_z, to_y, to_core):
        return (to_xh * (NZ * NY) + to_z * NY + to_y, chip * 2 + to_core)

    left = at(xh, z, (y + NY - 1) % NY, core)
    right = at(xh, z, (y + 1) % NY, core)
    opposite = at(xh, z, (y + 2) % NY, core)
    sibling = at(xh, z, y, 1 - core)
    partner = at(xh, z + 1 - 2 * parity, y, 1 - core)
    across = (seq, (1 - chip) * 2 + core)

    barrier = pltpu.get_barrier_semaphore()

    def greet(device):
        pl.semaphore_signal(barrier, inc=1, device_id=device, device_id_type=MESH)

    for device in (left, right, opposite, across):
        greet(device)
    for half in range(NX):
        for index in range(PAIRS):
            greet(at(half, 2 * index + 1 - core, y, parity))
            for to_core in range(2):

                @pl.when((half != xh) | (2 * index + core != z) | (to_core != core))
                def _():
                    greet(at(half, 2 * index + core, y, to_core))

    greeted = 4 + 3 * NX * PAIRS - jnp.where(home, 1, 0)

    def weight_copy(part):
        return pltpu.make_async_copy(
            w_ref.at[:, pl.ds(part * WIDTH, WIDTH)], w.at[part], w_sem.at[part]
        )

    staged = (
        (kc_hbm, kc_ref),
        (vc_hbm, vc_ref),
        (scale_hbm, scale_ref),
        (doc_hbm, doc_ref),
        (turn_hbm, turn_ref),
    )
    stage = [
        pltpu.make_async_copy(source, target, in_sem.at[index])
        for index, (source, target) in enumerate(staged)
    ]
    for copy in stage:
        copy.start()
    for copy in stage[:3]:
        copy.wait()

    own[0] = (kc_ref[...].astype(jnp.float32) * scale_ref[0]).astype(jnp.bfloat16)
    own[1] = (vc_ref[...].astype(jnp.float32) * scale_ref[1]).astype(jnp.bfloat16)

    @pl.when(home)
    def _():
        kv[UP, pair, y, core, parity] = own[core]

    pl.semaphore_wait(barrier, greeted)

    def column_copy(stream, step, half):
        to_xh, to_pair = (xh, pair + step) if stream == UP else (1 - xh, pair - step)
        return pltpu.make_async_remote_copy(
            src_ref=own.at[half],
            dst_ref=kv.at[stream, pair, y, half, parity],
            send_sem=send_z.at[stream, step, half],
            recv_sem=recv_z.at[stream, pair, parity],
            device_id=at(to_xh, (2 * to_pair + core + NZ) % NZ, y, half),
            device_id_type=MESH,
        )

    def arrival(stream, source, source_parity):
        return pltpu.make_async_remote_copy(
            src_ref=own.at[0],
            dst_ref=kv.at[stream, source, y, core, source_parity],
            send_sem=send_z.at[stream, 0, 0],
            recv_sem=recv_z.at[stream, source, source_parity],
            device_id=sibling,
            device_id_type=MESH,
        )

    def part_of(index):
        return pl.ds(index * HEADS * HEAD_DIM, min(HEADS, GROUPS - index * HEADS) * HEAD_DIM)

    swapped = [(mask_hbm, mask_ref), (q_hbm, q_ref)]
    swapped += [
        (result.at[:, part_of(index)], attended.at[:, part_of(index)]) for index in range(PARTS)
    ]

    def swap_copy(index):
        source, target = swapped[index]
        return pltpu.make_async_remote_copy(
            src_ref=source,
            dst_ref=target,
            send_sem=swap_send.at[index],
            recv_sem=swap_recv.at[index],
            device_id=partner,
            device_id_type=MESH,
        )

    def local_copy(index):
        source, target = swapped[index]
        return pltpu.make_async_copy(source, target, in_sem.at[len(staged) + index])

    def y_copy(stream, source, column, target, side):
        return pltpu.make_async_remote_copy(
            src_ref=kv.at[stream, source, column, core],
            dst_ref=kv.at[stream, source, column, core],
            send_sem=send_y.at[stream, source, side],
            recv_sem=recv_y.at[stream, source, side],
            device_id=target,
            device_id_type=MESH,
        )

    def core_copy(stream, source, column, side, half):
        return pltpu.make_async_remote_copy(
            src_ref=kv.at[stream, source, column, half],
            dst_ref=kv.at[stream, source, column, half],
            send_sem=send_core.at[stream, source, side],
            recv_sem=recv_core.at[stream, source, side],
            device_id=sibling,
            device_id_type=MESH,
        )

    y_left = (y + NY - 1) % NY
    y_right = (y + 1) % NY
    y_far = (y + 2) % NY

    sides = ((right, y_left), (left, y_right), (opposite, y_far))
    columns = (y_left, y_right, y_far, y)

    def active(stream, step):
        if stream == UP:
            return (step >= 0) & (step <= pair), pair - step
        return (xh == 1) & (step >= 0) & (step < PAIRS - pair), pair + step

    def column_send(step, act):
        for half in range(2):

            @pl.when((xh == 0) & (step <= pair))
            def _():
                act(column_copy(DOWN, step, half))

            @pl.when((pair + step < PAIRS) & ((step > 0) | (core != parity) | (core != half)))
            def _():
                act(column_copy(UP, step, half))

    def forward(stream, step):
        on, source = active(stream, step)

        @pl.when(on)
        def _():
            for source_parity in range(2):
                if stream == UP:

                    @pl.when((step > 0) | (core != parity) | (core != source_parity))
                    def _():
                        arrival(stream, source, source_parity).wait_recv()
                else:
                    arrival(stream, source, source_parity).wait_recv()
            for side in (2, 0, 1):
                y_copy(stream, source, y, sides[side][0], side).start()
            core_copy(stream, source, y, 3, core).start()

    for step in range(WINDOW):
        column_send(step, lambda copy: copy.start())

    def share(stream, step):
        on, source = active(stream, step)

        @pl.when(on)
        def _():
            for side, (target, column) in enumerate(sides):
                y_copy(stream, source, column, target, side).wait_recv()
                core_copy(stream, source, column, side, core).start()

    def drain(stream, step):
        on, source = active(stream, step)

        @pl.when(on)
        def _():
            for side, (target, _) in enumerate(sides):
                y_copy(stream, source, y, target, side).wait_send()
            for side, column in enumerate(columns):
                core_copy(stream, source, column, side, core).wait_send()

    forward(UP, 0)
    forward(DOWN, 0)
    if WINDOW < PAIRS:
        column_send(WINDOW, lambda copy: copy.start())

    @pl.when(home)
    def _():
        for index in range(2):
            local_copy(index).start()

    @pl.when(core != parity)
    def _():
        for index in range(2):
            swap_copy(index).start()

    for part in range(NHEAD):
        weight_copy(part).start()

    for copy in stage[3:]:
        copy.wait()

    lanes = lax.broadcasted_iota(jnp.int32, (1, BLOCK), 1)
    places = query_seq * BLOCK + lanes
    doc_start = jnp.zeros((1, BLOCK), jnp.int32)
    end = doc_ref[0]
    for index in range(doc_ref.shape[0]):
        doc_start = jnp.where(places >= end, end, doc_start)
        if index + 1 < doc_ref.shape[0]:
            end = end + doc_ref[index + 1]
    own_turns = turn_ref[pl.ds(query_seq, 1), :]
    earlier = jnp.zeros((1, BLOCK), jnp.int32)
    for back in range(3):
        block = jnp.maximum(query_seq - back, 0)
        turns = turn_ref[pl.ds(block, 1), :].astype(jnp.float32)
        column = jnp.transpose(jnp.broadcast_to(turns, (BLOCK, BLOCK))).astype(jnp.int32)
        count = jnp.sum(jnp.where(column < own_turns, 1, 0), axis=0, keepdims=True)
        earlier = earlier + jnp.where(query_seq >= back, count, 0)
    turn_start = jnp.maximum(query_seq - 2, 0) * BLOCK + earlier

    def along_rows(row):
        wide = jnp.broadcast_to(row.astype(jnp.float32), (BLOCK, BLOCK))
        return jnp.transpose(wide).astype(jnp.int32)

    starts[0] = along_rows(doc_start)
    starts[1] = along_rows(turn_start)
    key_lanes = lax.broadcasted_iota(jnp.int32, (BLOCK, BLOCK), 1)
    mask_lanes = lax.broadcasted_iota(jnp.int32, mask_ref.shape, 1)
    query_places = query_seq * BLOCK + lax.broadcasted_iota(jnp.int32, (BLOCK, BLOCK), 0)

    best[...] = jnp.full_like(best, MASKED)
    summed[...] = jnp.zeros_like(summed)

    def divide(index, target):
        for group in range(index * HEADS, min((index + 1) * HEADS, GROUPS)):
            rows = slice(group * BLOCK, (group + 1) * BLOCK)
            target[:, group * HEAD_DIM : (group + 1) * HEAD_DIM] = (
                summed[rows, :HEAD_DIM] / summed[rows, HEAD_DIM:]
            ).astype(jnp.bfloat16)

    def attend_pair(stream, source, leaving):
        for side, column in enumerate(columns):
            core_copy(stream, source, column, side, 1 - core).wait_recv()
        for index in range(2 * NY):
            block = (source * 2 + index // NY) * NY + index % NY
            if stream == UP:
                block = block + xh * (NZ * NY)
            kept = jnp.sum(
                jnp.where(mask_lanes == block, mask_ref[...], 0), axis=1, keepdims=True
            )
            same = jnp.where(block == query_seq, 1, 0)
            low = jnp.maximum(starts[0], starts[1] * (1 - jnp.maximum(kept, same)))
            places = block * BLOCK + key_lanes
            allowed = (places >= low) & (places <= query_places)
            bias[:, pl.ds(index * BLOCK, BLOCK)] = jnp.where(allowed, 0.0, MASKED)
        blocks = [(index % NY, index // NY) for index in range(2 * NY)]
        keys = jnp.concatenate([kv[stream, source, c, 0, r] for c, r in blocks], axis=0)
        values = jnp.concatenate([kv[stream, source, c, 1, r] for c, r in blocks], axis=0)
        values = jnp.concatenate([values, jnp.ones_like(values)], axis=1)
        for start in range(0, GROUPS, HEADS):
            heads = min(HEADS, GROUPS - start)
            rows = pl.ds(start * BLOCK, heads * BLOCK)
            scores = lax.dot_general(
                q_rows[rows, :],
                keys,
                (((1,), (1,)), ((), ())),
                preferred_element_type=jnp.float32,
            )
            scores = scores.reshape(heads, BLOCK, 2 * NY * BLOCK) + bias[...][None]
            scores = scores.reshape(heads * BLOCK, 2 * NY * BLOCK)
            previous = best[rows, :]
            newest = jnp.maximum(previous, jnp.max(scores, axis=1, keepdims=True))
            factor = jnp.exp2((previous - newest) * FACTOR)
            weights = jnp.exp2((scores - newest) * FACTOR)
            best[rows, :] = newest
            summed[rows, :] = summed[rows, :] * factor + jnp.dot(
                weights.astype(jnp.bfloat16), values, preferred_element_type=jnp.float32
            )
            if leaving:
                divide(start // HEADS, result)
                swap_copy(2 + start // HEADS).start()

    def attend(stream, step):
        on, source = active(stream, step)
        down_last = (xh == 1) & (PAIRS - 1 - pair >= pair)
        if stream == UP:
            last = (step == pair) & jnp.logical_not(down_last)
        else:
            last = (step == PAIRS - 1 - pair) & down_last
        leaving = last & (core != parity)

        @pl.when(on & jnp.logical_not(leaving))
        def _():
            attend_pair(stream, source, False)

        @pl.when(on & leaving)
        def _():
            attend_pair(stream, source, True)

    def take_queries():
        @pl.when(home)
        def _():
            for index in range(2):
                local_copy(index).wait()

        @pl.when(core != parity)
        def _():
            for index in range(2):
                swap_copy(index).wait_recv()

        for group in range(GROUPS):
            rows = slice(group * BLOCK, (group + 1) * BLOCK)
            q_rows[rows, :] = q_ref[:, group * HEAD_DIM : (group + 1) * HEAD_DIM]

    def advance(step, carry):
        @pl.when(step > 0)
        def _():
            forward(UP, step)
            forward(DOWN, step)
            if WINDOW < PAIRS:
                column_send(step + WINDOW, lambda copy: copy.start())

        @pl.when(step == ATTEND_LAG)
        def _():
            take_queries()

        attend(UP, step - ATTEND_LAG)
        attend(DOWN, step - ATTEND_LAG)
        share(UP, step - SHARE_LAG)
        share(DOWN, step - SHARE_LAG)
        return carry

    lax.fori_loop(0, PAIRS + ATTEND_LAG, advance, 0)

    @pl.when(home)
    def _():
        for index in range(PARTS):
            divide(index, attended)

    @pl.when(core != parity)
    def _():
        for index in range(PARTS):
            swap_copy(2 + index).wait_recv()

    for part in range(NHEAD):
        weight_copy(part).wait()

    def project(part, start, width):
        return jnp.dot(
            attended[...],
            w[part, :, pl.ds(start, width)],
            preferred_element_type=jnp.float32,
        )

    def sibling_copy(index):
        start, width = CHUNKS[index % len(CHUNKS)]
        place = index // len(CHUNKS)
        return pltpu.make_async_remote_copy(
            src_ref=rs_out.at[place, :, pl.ds(start, width)],
            dst_ref=rs_in.at[place, :, pl.ds(start, width)],
            send_sem=rs_send.at[index],
            recv_sem=rs_recv.at[index],
            device_id=sibling,
            device_id_type=MESH,
        )

    def cross_copy(index):
        start, width = CHUNKS[index]
        return pltpu.make_async_remote_copy(
            src_ref=cross_out.at[:, pl.ds(start, width)],
            dst_ref=cross_in.at[:, pl.ds(start, width)],
            send_sem=cross_send.at[index],
            recv_sem=cross_recv.at[index],
            device_id=across,
            device_id_type=MESH,
        )

    far = 1 - chip
    for index, (start, width) in enumerate(CHUNKS):
        rs_out[0, :, pl.ds(start, width)] = project(far * 2 + 1 - core, start, width).astype(
            jnp.bfloat16
        )
        sibling_copy(index).start()
    for index, (start, width) in enumerate(CHUNKS):
        mine = project(far * 2 + core, start, width)
        sibling_copy(index).wait_recv()
        cross_out[:, pl.ds(start, width)] = (
            mine + rs_in[0, :, pl.ds(start, width)].astype(jnp.float32)
        ).astype(jnp.bfloat16)
        cross_copy(index).start()
    for index, (start, width) in enumerate(CHUNKS):
        rs_out[1, :, pl.ds(start, width)] = project(chip * 2 + 1 - core, start, width).astype(
            jnp.bfloat16
        )
        sibling_copy(len(CHUNKS) + index).start()
    for index, (start, width) in enumerate(CHUNKS):
        mine = project(head, start, width)
        sibling_copy(len(CHUNKS) + index).wait_recv()
        mine = mine + rs_in[1, :, pl.ds(start, width)].astype(jnp.float32)
        cross_copy(index).wait_recv()
        out_ref[:, pl.ds(start, width)] = (
            mine + cross_in[:, pl.ds(start, width)].astype(jnp.float32)
        ).astype(jnp.bfloat16)

    for index in range(2 * len(CHUNKS)):
        sibling_copy(index).wait_send()
    for index in range(len(CHUNKS)):
        cross_copy(index).wait_send()

    def finish(step, carry):
        drain(UP, step)
        drain(DOWN, step)
        return carry

    lax.fori_loop(0, PAIRS, finish, 0)
    for step in range(PAIRS):
        column_send(step, lambda copy: copy.wait_send())

    @pl.when(core != parity)
    def _():
        for index in range(2 + PARTS):
            swap_copy(index).wait_send()


def on_device(
    queries, key_codes, value_codes, kv_scales, out_weight, turn_ids, block_mask, doc_lengths
):
    dma = pltpu.SemaphoreType.DMA
    return pl.pallas_call(
        kernel,
        out_shape=jax.ShapeDtypeStruct(queries.shape, jnp.bfloat16),
        in_specs=[pl.BlockSpec(memory_space=pltpu.HBM)] * 8,
        out_specs=pl.BlockSpec(memory_space=pltpu.VMEM),
        scratch_shapes=[
            pltpu.VMEM(queries.shape, jnp.bfloat16),
            pltpu.VMEM(key_codes.shape, jnp.bfloat16),
            pltpu.VMEM(value_codes.shape, jnp.bfloat16),
            pltpu.SMEM((2,), jnp.float32),
            pltpu.VMEM((turn_ids.shape[0] // BLOCK, BLOCK), jnp.int32),
            pltpu.VMEM(block_mask.shape, jnp.int32),
            pltpu.SMEM(doc_lengths.shape, jnp.int32),
            pltpu.VMEM((2, BLOCK, HEAD_DIM), jnp.bfloat16),
            pltpu.VMEM((2, PAIRS, NY, 2, 2, BLOCK, HEAD_DIM), jnp.bfloat16),
            pltpu.VMEM((GROUPS * BLOCK, HEAD_DIM), jnp.bfloat16),
            pltpu.VMEM((NHEAD, WIDTH, WIDTH), jnp.bfloat16),
            pltpu.VMEM((BLOCK, 2 * NY * BLOCK), jnp.float32),
            pltpu.VMEM((2, BLOCK, BLOCK), jnp.int32),
            pltpu.VMEM((GROUPS * BLOCK, 1), jnp.float32),
            pltpu.VMEM((GROUPS * BLOCK, 2 * HEAD_DIM), jnp.float32),
            pltpu.VMEM((BLOCK, WIDTH), jnp.bfloat16),
            pltpu.VMEM((BLOCK, WIDTH), jnp.bfloat16),
            pltpu.VMEM((2, BLOCK, WIDTH), jnp.bfloat16),
            pltpu.VMEM((2, BLOCK, WIDTH), jnp.bfloat16),
            pltpu.VMEM((BLOCK, WIDTH), jnp.bfloat16),
            pltpu.VMEM((BLOCK, WIDTH), jnp.bfloat16),
            dma((NHEAD,)),
            dma((7,)),
            dma((2, PAIRS, 2)),
            dma((2, PAIRS, 2)),
            dma((2, PAIRS, 3)),
            dma((2, PAIRS, 3)),
            dma((2, PAIRS, 4)),
            dma((2, PAIRS, 4)),
            dma((2 + PARTS,)),
            dma((2 + PARTS,)),
            dma((2 * len(CHUNKS),)),
            dma((2 * len(CHUNKS),)),
            dma((len(CHUNKS),)),
            dma((len(CHUNKS),)),
        ],
        compiler_params=pltpu.CompilerParams(
            collective_id=0, has_side_effects=True, vmem_limit_bytes=40 * 1024 * 1024
        ),
    )(
        *(
            pltpu.with_memory_space_constraint(operand, pltpu.HBM)
            for operand in (
                queries,
                key_codes,
                value_codes,
                kv_scales.reshape(2),
                out_weight,
                turn_ids.reshape(-1, BLOCK),
                block_mask,
                doc_lengths,
            )
        )
    )


def solution(mesh):
    placed = (
        P("seq", "head"),
        P("seq", "head"),
        P("seq", "head"),
        P(None, "seq", "head"),
        P("head", None),
        P(),
        P("seq", None),
        P(),
    )
    return jax.shard_map(
        on_device, mesh=mesh, in_specs=placed, out_specs=P("seq", "head"), check_vma=False
    )
```
